32 devices in a mesh: space: 8 (over y, x, core), mode: 4 (over z).
Axes of the slice: x: 2, y: 2, z: 4, core: 2. Of those that a mesh axis runs over, the one named last changes fastest.
Arguments:
- modes: bfloat16 [512, 96, 2048], P('mode', 'space'), may hold values from -6 to 6
- phases: int32 [96, 2048], P('space'), may hold values from 0 to 2
- velocity: float32 [3], replicated, may hold values from 0.5 to 1.5
Outputs:
- reduced: float32 [512, 512], P('space', 'mode')
The draws below stay inside these ranges and needn't reach their ends.
All inputs are finite; a program needn't handle non-finite values.
Results may differ from the reference program's by a relative error of at most 0.0028.
Values may be sent and summed in bfloat16 or wider, within the bound.
No kernel may reach another device: no remote copies, remote signals or barrier semaphores. Data moves between devices by JAX's collectives and lax.ppermute only.
A program may use at most 192 MiB of HBM per device.

```python
import math
import jax
import jax.numpy as jnp
from jax import lax

MODES = 512
NZ = 64
PLANE = 2048
NX = 96


def with_ends(values, rng, least, top_value):
    longest = values.shape.index(max(values.shape))
    spots = []
    for shift in (0, 1):
        where = [jax.random.randint(jax.random.fold_in(rng, axis), (), 0, length) for axis, length in enumerate(values.shape)]
        where[longest] = (where[longest] + shift) % values.shape[longest]
        spots.append(tuple(where))
    return values.at[spots[0]].set(least).at[spots[1]].set(top_value)


def steps_of(stream_key, dims, split, least, largest):
    loudness, own = 1.0, jax.random.fold_in(stream_key, 6)
    for dim, blocks in split:
        steps = jnp.exp(jax.random.uniform(jax.random.fold_in(own, dim), (blocks,), jnp.float32, least / len(split), largest / len(split)))
        loudness = loudness * jnp.repeat(steps, dims[dim] // blocks).reshape([-1 if axis == dim else 1 for axis in range(len(dims))])
    return loudness


def centred(stream_key, extent, scale, most, split=(), held_as=jnp.bfloat16):
    drawn = scale * jax.random.normal(stream_key, extent, jnp.float32)
    if split:
        drawn = drawn * steps_of(stream_key, extent, split, -0.22, 0.18)
    return jnp.clip(drawn, -most, most).astype(held_as)


def setup_inputs(seed: int = 0) -> dict:
    key_list = jax.random.split(jax.random.key(seed), 4)
    return {
        "modes": centred(key_list[0], (MODES, NX, PLANE), 1.0, 6.0, ((0, 4), (1, 8))),
        "phases": with_ends(jax.random.randint(key_list[1], (NX, PLANE), 0, 3), jax.random.fold_in(key_list[1], 1), 0, 2).astype(jnp.int32),
        "velocity": jnp.clip(jax.random.uniform(key_list[2], (3,), jnp.float32, 0.5, 1.5), 0.5, 1.5),
    }


def shifted(field, offset):
    width = field.shape[-1]
    zeros_part = jnp.zeros(field.shape[:-1] + (abs(offset),), jnp.float32)
    if offset > 0:
        return jnp.concatenate([field[..., offset:], zeros_part], axis=-1)
    return jnp.concatenate([zeros_part, field[..., :width + offset]], axis=-1)

def apply_block(block, weight, velocity, eps):
    padded = jnp.pad(block.astype(jnp.float32), ((0, 0), (1, 1), (0, 0)))
    center = padded[:, 1:-1]
    x_up = padded[:, 2:]
    x_down = padded[:, :-2]
    zpos = lax.broadcasted_iota(jnp.int32, (1, 1, center.shape[-1]), 2) % NZ
    z_up = jnp.where(zpos == NZ - 1, 0.0, shifted(center, 1))
    z_down = jnp.where(zpos == 0, 0.0, shifted(center, -1))
    y_up = shifted(center, NZ)
    y_down = shifted(center, -NZ)
    spread = x_up + x_down + y_up + y_down + z_up + z_down - 6.0 * center
    drift = velocity[0] * (x_up - x_down) + velocity[1] * (y_up - y_down) + velocity[2] * (z_up - z_down)
    return (weight[None] * (eps * spread - 0.5 * drift)).astype(jnp.bfloat16)

def reference(modes, phases, velocity):
    weight = jnp.where(phases == 0, 0.1, jnp.where(phases == 1, 1.0, 0.5)).astype(jnp.float32)
    eps = 1.0 / math.sqrt(NX * PLANE)
    blocks = modes.reshape(MODES // 16, 16, NX, PLANE)
    applied = lax.map(lambda blk: apply_block(blk, weight, velocity, eps), blocks)
    applied = applied.reshape(MODES, NX * PLANE)
    flat = modes.reshape(MODES, NX * PLANE)
    total = lax.dot_general(flat, applied, (((1,), (1,)), ((), ())), preferred_element_type=jnp.float32)
    return total * eps
```

```python
import functools
import math

import jax
import jax.numpy as jnp
from jax import lax
from jax.experimental import pallas as pl
from jax.experimental.pallas import tpu as pltpu
from jax.sharding import PartitionSpec as P

NZ = 64
LANES = 128
SUB = 16
BF = jnp.bfloat16
F32 = jnp.float32


def cyclic(devices, k):
    return [(i, (i + k) % devices) for i in range(devices)]


def product(left, right):
    return lax.dot_general(left, right, (((1,), (1,)), ((), ())), preferred_element_type=F32)


def phase_kernel(n_old, eps, steps, keep, velocity, w, wh, x, xp, xn, xd, xu, h, *refs):
    old = [refs[4 * i : 4 * i + 4] for i in range(n_old)]
    out = refs[4 * n_old :]
    if keep:
        a, ah = out[0], out[1]
        sums = out[2:]
    else:
        sums, (a, ah) = out[:-2], out[-2:]
    i = pl.program_id(0)
    count, tiles = x.shape[1], x.shape[2] // LANES
    v0, v1, v2 = velocity[0], velocity[1], velocity[2]
    lane = lax.broadcasted_iota(jnp.int32, (SUB, LANES), 1)
    low = lane < NZ
    at_end = (lane % NZ) == NZ - 1
    at_start = (lane % NZ) == 0

    def body(j, carry):
        rows = pl.ds(pl.multiple_of(j * SUB, SUB), SUB)

        def tile(ref, r, t):
            return ref[r, rows, t * LANES : (t + 1) * LANES].astype(F32)

        halo = h[0, rows, :].astype(F32)
        swapped = pltpu.roll(halo, NZ, 1)
        center = [[tile(x, r, t) for t in range(tiles)] for r in (0, 1)]
        tails = []
        for r in (0, 1):
            turned = [pltpu.roll(c, NZ, 1) for c in center[r]]
            tails.append((center[r][-1], turned[-1]))
            for t in range(tiles):
                c = center[r][t]
                if r == 0:
                    x_up = center[1][t]
                    x_down = jnp.where(i == 0, tile(xd, 0, t), tile(xp, 0, t))
                else:
                    x_up = jnp.where(i == steps - 1, tile(xu, 0, t), tile(xn, 0, t))
                    x_down = center[0][t]
                after = turned[t + 1] if t + 1 < tiles else (swapped if r == 0 else halo)
                before = turned[t - 1] if t > 0 else jnp.zeros_like(c)
                y_up = jnp.where(low, turned[t], after)
                y_down = jnp.where(low, before, turned[t])
                z_up = jnp.where(at_end, 0.0, pltpu.roll(c, LANES - 1, 1))
                z_down = jnp.where(at_start, 0.0, pltpu.roll(c, 1, 1))
                spread = x_up + x_down + y_up + y_down + z_up + z_down - 6.0 * c
                drift = v0 * (x_up - x_down) + v1 * (y_up - y_down) + v2 * (z_up - z_down)
                weight = w[r, :, t * LANES : (t + 1) * LANES]
                a[r, rows, t * LANES : (t + 1) * LANES] = (
                    weight * (eps * spread - 0.5 * drift)
                ).astype(BF)
        below = jnp.where(low, tails[0][1], tails[1][0])
        ah[0, rows, :] = (wh[0] * (eps * below + 0.5 * (v1 * below))).astype(BF)
        return carry

    lax.fori_loop(0, count // SUB, body, 0)

    @pl.when(i == 0)
    def _():
        for s in sums:
            s[...] = jnp.zeros_like(s)

    for o, (ox, oh, oa, oah) in enumerate(old):
        sums[2 * o][...] += product(x[0], oa[0]) + product(x[1], oa[1]) + product(h[0], oah[0])
        sums[2 * o + 1][...] += product(ox[0], a[0]) + product(ox[1], a[1]) + product(oh[0], ah[0])
    sums[2 * n_old][...] += product(x[0], a[0]) + product(x[1], a[1]) + product(h[0], ah[0])


def phase(velocity, w, wh, new, old, eps, keep):
    x, xd, xu, h = new
    rows, count, width = x.shape
    steps = rows // 2
    pair = lambda m: pl.BlockSpec((2, m, width), lambda i: (i, 0, 0))
    single = lambda f: pl.BlockSpec((1, count, width), lambda i: (f(i), 0, 0))
    halo = lambda m: pl.BlockSpec((1, m, LANES), lambda i: (i, 0, 0))
    specs = [
        pl.BlockSpec(memory_space=pltpu.SMEM),
        pl.BlockSpec((2, 1, width), lambda i: (i, 0, 0)),
        pl.BlockSpec((1, 1, LANES), lambda i: (i, 0, 0)),
        pair(count),
        single(lambda i: jnp.maximum(2 * i - 1, 0)),
        single(lambda i: jnp.minimum(2 * i + 2, rows - 1)),
        single(lambda i: 0),
        single(lambda i: 0),
        halo(count),
    ]
    args = [velocity, w, wh, x, x, x, xd, xu, h]
    sums = []
    for ox, oh, oa, oah in old:
        m = ox.shape[1]
        specs += [pair(m), halo(m), pair(m), halo(m)]
        args += [ox, oh, oa, oah]
        sums += [(count, m), (m, count)]
    sums.append((count, count))
    out_shape = [jax.ShapeDtypeStruct(s, F32) for s in sums]
    out_specs = [pl.BlockSpec(s, lambda i: (0, 0)) for s in sums]
    scratch = []
    if keep:
        out_shape = [
            jax.ShapeDtypeStruct(x.shape, BF),
            jax.ShapeDtypeStruct(h.shape, BF),
        ] + out_shape
        out_specs = [pair(count), halo(count)] + out_specs
    else:
        scratch = [pltpu.VMEM((2, count, width), BF), pltpu.VMEM((1, count, LANES), BF)]
    elements = rows * count * width
    pairs = sum(a * b for a, b in sums)
    outs = pl.pallas_call(
        functools.partial(phase_kernel, len(old), eps, steps, keep),
        grid=(steps,),
        in_specs=specs,
        out_specs=out_specs,
        out_shape=out_shape,
        scratch_shapes=scratch,
        compiler_params=pltpu.CompilerParams(vmem_limit_bytes=32 << 20),
        cost_estimate=pl.CostEstimate(
            flops=25 * elements + 2 * pairs * rows * width,
            bytes_accessed=6 * elements + 4 * sum(o[0].size for o in old) + 4 * pairs,
            transcendentals=0,
        ),
    )(*args)
    if keep:
        return (x, h, outs[0], outs[1]), outs[2:]
    return None, outs


def local(modes, phases, velocity):
    space, n = lax.axis_size("space"), lax.axis_size("mode")
    sp, q = lax.axis_index("space"), lax.axis_index("mode")
    count, rows, plane = modes.shape
    width = plane // n
    eps = 1.0 / math.sqrt(space * rows * plane)
    field = jnp.transpose(modes, (1, 0, 2))

    weight = jnp.where(phases == 0, 0.1, jnp.where(phases == 1, 1.0, 0.5)).astype(F32)
    w = lax.dynamic_slice_in_dim(weight, q * width, width, axis=1)[:, None, :]
    after = jnp.minimum((q + 1) * width, plane - NZ)
    wh = lax.dynamic_slice_in_dim(weight, after, NZ, axis=1).reshape(rows // 2, 1, LANES)

    def slab(owner):
        return lax.dynamic_slice_in_dim(field, owner * width, width, axis=2)

    def line(owner):
        start = jnp.minimum((owner + 1) * width, plane - NZ)
        part = lax.dynamic_slice_in_dim(field, start, NZ, axis=2)
        part = jnp.where(owner == n - 1, jnp.zeros_like(part), part)
        return jnp.concatenate([part[0::2], part[1::2]], axis=-1)

    order = [0, 1, 3, 2] if n == 4 else list(range(n))
    xs, hs = {}, {}
    for k in order:
        s, l = slab((q + k) % n), line((q + k) % n)
        xs[k] = lax.ppermute(s, "mode", cyclic(n, k)) if k else s
        hs[k] = lax.ppermute(l, "mode", cyclic(n, k)) if k else l
    groups = [[k] for k in order] if n == 4 else [order]
    up = [(i, i + 1) for i in range(space - 1)]
    down = [(i + 1, i) for i in range(space - 1)]
    old, found, names = [], {}, []
    for g, group in enumerate(groups):
        join = lambda parts: parts[0] if len(parts) == 1 else jnp.concatenate(parts, axis=1)
        x, h = join([xs[k] for k in group]), join([hs[k] for k in group])
        xd = lax.ppermute(x[rows - 1 :], "space", up)
        xu = lax.ppermute(x[:1], "space", down)
        kept, sums = phase(velocity, w, wh, (x, xd, xu, h), old, eps, g + 1 < len(groups))
        for o, name in enumerate(names):
            found[g, name], found[name, g] = sums[2 * o], sums[2 * o + 1]
        found[g, g] = sums[-1]
        names.append(g)
        old.append(kept)

    if n == 4:
        place = [order.index((n - d) % n) for d in range(n)]
        total = jnp.concatenate(
            [jnp.concatenate([found[a, b] for b in place], axis=1) for a in place], axis=0
        )
    else:
        only = found[0, 0].reshape(n, count, n, count)
        turn = jnp.array([(n - d) % n for d in range(n)])
        total = only[turn][:, :, turn].reshape(n * count, n * count)
    size = n * count
    share = size // space

    def piece(target):
        return lax.dynamic_slice_in_dim(total, (target * share - q * count) % size, share, axis=0)

    mine = piece(sp)
    for k in range(1, space):
        mine = mine + lax.ppermute(piece((sp + k) % space), "space", cyclic(space, k))
    result = mine[:, :count]
    for k in range(1, n):
        result = result + lax.ppermute(mine[:, k * count : (k + 1) * count], "mode", cyclic(n, k))
    return result * eps


def solution(mesh):
    placed = (P("mode", "space", None), P("space", None), P())
    return jax.shard_map(
        local, mesh=mesh, in_specs=placed, out_specs=P("space", "mode"), check_vma=False
    )
```

```python
import functools
import math

import jax
import jax.numpy as jnp
from jax import lax
from jax.experimental import pallas as pl
from jax.experimental.pallas import tpu as pltpu
from jax.sharding import PartitionSpec as P

NZ = 64
LANES = 128
SUB = 16
BF = jnp.bfloat16
F32 = jnp.float32
VMEM = pltpu.VMEM


def product(left, right):
    return lax.dot_general(left, right, (((1,), (1,)), ((), ())), preferred_element_type=F32)


def apply_rows(i, eps, velocity, w, wh, xs, h, a, tiles, rows, off, count, flip):
    span = rows + 2
    xp, xm = eps - 0.5 * velocity[0], eps + 0.5 * velocity[0]
    yp, ym = eps - 0.5 * velocity[1], eps + 0.5 * velocity[1]
    zp, zm = eps - 0.5 * velocity[2], eps + 0.5 * velocity[2]
    lane = lax.broadcasted_iota(jnp.int32, (SUB, LANES), 1)
    low = lane < NZ
    zps = jnp.where(lane % NZ == NZ - 1, 0.0, zp)
    zms = jnp.where(lane % NZ == 0, 0.0, zm)
    own = jnp.where(low, yp, ym)
    other = jnp.where(low, ym, yp)
    at_end = jnp.where(flip == 0, 1.0, 0.0)
    at_start = 1.0 - at_end

    def body(j, carry):
        start = pl.multiple_of(j * SUB, SUB)
        source = pl.ds(start, SUB)
        target = pl.ds(pl.multiple_of(j * SUB + off, SUB), SUB)
        halo = h(i, source).astype(F32)
        ends = (pltpu.roll(halo, NZ, 1), halo)
        starts = (halo, pltpu.roll(halo, NZ, 1))
        center = [
            [xs[t * span + 2 * i + r, source, :].astype(F32) for t in range(tiles)] for r in range(4)
        ]
        firsts, lasts = [], []
        for r in (0, 1):
            mid = center[r + 1]
            turned = [pltpu.roll(c, NZ, 1) for c in mid]
            lasts.append(turned[-1] if r == 0 else mid[-1])
            firsts.append(mid[0] if r == 0 else turned[0])
            for t in range(tiles):
                c = mid[t]
                behind = turned[t + 1] if t + 1 < tiles else at_end * ends[r]
                before = turned[t - 1] if t > 0 else at_start * starts[r]
                value = xp * center[r + 2][t] + xm * center[r][t]
                value = value + own * turned[t] + other * jnp.where(low, before, behind)
                value = value + zps * pltpu.roll(c, LANES - 1, 1) + zms * pltpu.roll(c, 1, 1)
                value = (value - (6.0 * eps) * c) * w[2 * i + r, :, t * LANES : (t + 1) * LANES]
                a[t * rows + 2 * i + r, target, :] = value.astype(BF)
        last = jnp.where(low, lasts[0], lasts[1])
        first = jnp.where(low, firsts[0], firsts[1])
        side = at_end * ym * last + at_start * yp * first
        a[tiles * rows + i, target, :] = (wh[i] * side).astype(BF)
        return carry

    lax.fori_loop(0, count // SUB, body, 0)


def phase_kernel(cfg, *refs):
    refs = list(refs)
    d, off, count, whole = cfg["d"], cfg["off"], cfg["count"], cfg["whole"]
    rows, tiles = cfg["rows"], cfg["tiles"]
    steps, end, mine, span = rows // 2, off + count, slice(off, off + count), rows + 2
    last, part = cfg["last"], count < whole
    take = lambda k: [refs.pop(0) for _ in range(k)]
    order, velocity, w, wh, xd, xu = take(6)
    parts = take(cfg["n_parts"])
    old = [take(2) for _ in range(cfg["n_old"])]
    prev = take(2) if cfg["prev"] else None
    gin = take(1)[0] if cfg["gin"] else None
    xo = take(1)[0] if part and not last else None
    a = None if last else take(1)[0]
    (gout,) = take(1)
    if last:
        (a,) = take(1)
    xs, t2 = take(2)
    t1 = take(1)[0] if cfg["t1"] else None
    g = take(1)[0] if last else gout

    edge = cfg["edge"]
    if part:
        rim, inner = parts[0], parts[-1]
        deep = rows - 2
        base = tiles * deep + (off // count) * (2 * tiles + rows // 2)
        halo_of = lambda i, at: rim[base + 2 * tiles + i, at, :]
        inside = slice(0, count)
    else:
        inside = mine
        halo_of = lambda i, at: parts[0][tiles * rows + i, at, :]
    for t in range(tiles):
        xs[t * span] = xd[edge + t]
        xs[t * span + rows + 1] = xu[edge + t]
        if part:
            xs[t * span + 1] = rim[base + 2 * t]
            xs[t * span + rows] = rim[base + 2 * t + 1]
            xs[t * span + 2 : t * span + rows] = inner[t * deep : (t + 1) * deep]
        else:
            xs[t * span + 1 : t * span + rows + 1] = parts[0][t * rows : (t + 1) * rows]
    t2[...] = jnp.zeros_like(t2)
    if t1 is not None:
        t1[...] = jnp.zeros_like(t1)
    if part:
        a[...] = jnp.zeros_like(a) if prev is None or last else prev[1][...]

    def padded(value, before=None):
        pieces = [value]
        if off:
            pieces.insert(0, jnp.zeros((off, LANES), BF) if before is None else before)
        if end < whole:
            pieces.append(jnp.zeros((whole - end, LANES), BF))
        return pieces[0] if len(pieces) == 1 else jnp.concatenate(pieces, axis=0)

    def body(i, carry):
        flip = order[1]
        apply_rows(
            i, cfg["eps"], velocity, w, wh, xs, halo_of, a, tiles, rows, off, count, flip
        )
        picks = [t * rows + 2 * i + r for r in (0, 1) for t in range(tiles)]
        picks.append(tiles * rows + i)
        wide = lambda ref: jnp.concatenate([ref[k] for k in picks], axis=1)
        new = [xs[t * span + 2 * i + r + 1] for r in (0, 1) for t in range(tiles)]
        new.append(halo_of(i, inside))
        if part:
            before = [None if prev is None else prev[0][k, :off, :] for k in picks]
            both = [padded(v, u) for v, u in zip(new, before)]
            if xo is not None:
                for k, v in zip(picks, both):
                    xo[k] = v
        else:
            both = new
        fresh = [padded(v) for v in new]
        mark = [padded(a[k, mine, :]) for k in picks]
        tall = [wide(ox) for ox, _ in old] + [jnp.concatenate(both, axis=1)]
        t2[...] += product(jnp.concatenate(tall, axis=0), jnp.concatenate(mark, axis=1))
        tall = [wide(oa) for _, oa in old] + ([wide(prev[1])] if prev is not None else [])
        if tall:
            t1[...] += product(jnp.concatenate(tall, axis=0), jnp.concatenate(fresh, axis=1))
        return carry

    lax.fori_loop(0, steps, body, 0)

    g[...] = jnp.zeros_like(g) if gin is None else gin[...]
    block = lambda k: slice(k * whole, (k + 1) * whole)
    names = [*cfg["old"], d]
    for k, o in enumerate(names):
        g[block(o), block(d)] += t2[block(k), :]
    for k, o in enumerate(names if prev is not None else names[:-1]):
        g[block(d), block(o)] += t1[block(k), :].T
    if last:
        q = order[0]
        n, space = cfg["n"], cfg["space"]
        share = gout.shape[1]
        per = whole // share
        for s in range(space):
            first = pl.multiple_of(((s // per) ^ q) * whole + (s % per) * share, share)
            for z in range(n):
                start = pl.multiple_of((z ^ q) * whole, whole)
                gout[s * n + z] = g[pl.ds(first, share), pl.ds(start, whole)].astype(BF)


def phase(cfg, order, velocity, w, wh, xd, xu, parts, old, prev, gin):
    rows, tiles, whole, count = cfg["rows"], cfg["tiles"], cfg["whole"], cfg["count"]
    size, last, part = cfg["n_blocks"] * whole, cfg["last"], count < whole
    kept = jax.ShapeDtypeStruct((tiles * rows + rows // 2, whole, LANES), BF)
    args = [order, velocity, w, wh, xd, xu, *parts]
    for group in [*old, *([prev] if prev is not None else [])]:
        args += list(group)
    if gin is not None:
        args.append(gin)
    scratch = []
    if last:
        gshape = jax.ShapeDtypeStruct((cfg["space"] * cfg["n"], size // cfg["space"], whole), BF)
        out_shape = [gshape]
        scratch.append(VMEM(kept.shape, BF))
    else:
        out_shape = [kept] * (2 if part else 1) + [jax.ShapeDtypeStruct((size, size), F32)]
    seconds = len(old) + (prev is not None)
    scratch.append(VMEM((tiles * (rows + 2), count, LANES), BF))
    scratch.append(VMEM(((len(old) + 1) * whole, whole), F32))
    if seconds:
        scratch.append(VMEM((seconds * whole, whole), F32))
    if last:
        scratch.append(VMEM((size, size), F32))
    elements = rows * count * tiles * LANES
    cfg = dict(cfg, n_parts=len(parts), n_old=len(old), prev=prev is not None, gin=gin is not None, t1=bool(seconds))
    vmem = pl.BlockSpec(memory_space=VMEM)
    smem = pl.BlockSpec(memory_space=pltpu.SMEM)
    outs = pl.pallas_call(
        functools.partial(phase_kernel, cfg),
        in_specs=[smem, smem] + [vmem] * (len(args) - 2),
        out_specs=[vmem] * len(out_shape),
        out_shape=out_shape,
        scratch_shapes=scratch,
        compiler_params=pltpu.CompilerParams(vmem_limit_bytes=cfg["vmem"] << 20),
        cost_estimate=pl.CostEstimate(
            flops=20 * elements + 4 * size * elements,
            bytes_accessed=6 * elements,
            transcendentals=0,
        ),
    )(*args)
    if last:
        return None, outs[0]
    return (outs[0] if part else parts[0], outs[-2]), outs[-1]


def pack_kernel(jobs, n, rows, tiles, order, field, *refs):
    outs = refs[: len(jobs)]
    line, packed, sem, line_sem, out_sem = refs[len(jobs) :]
    q, flip = order[0], order[1]
    copies, halos = [], []
    for k, (d, kind, a, b) in enumerate(jobs):
        owner = q ^ d
        base = owner * tiles * LANES
        cut = lambda t: pl.ds(pl.multiple_of(base + t * LANES, LANES), LANES)
        deep = rows - 2
        for t in range(tiles):
            if kind == "full":
                copies.append((field.at[:, :, cut(t)], outs[k].at[t * rows : (t + 1) * rows]))
                continue
            copies.append((field.at[1 : rows - 1, a:b, cut(t)], outs[k].at[t * deep : (t + 1) * deep]))
            if kind == "rim":
                for c in (0, 1):
                    first = tiles * deep + c * (2 * tiles + rows // 2)
                    half = slice(c * (b - a), (c + 1) * (b - a))
                    copies.append((field.at[0, half, cut(t)], outs[k].at[first + 2 * t]))
                    copies.append((field.at[rows - 1, half, cut(t)], outs[k].at[first + 2 * t + 1]))
        if kind == "full":
            halos.append((k, owner, rows * tiles, slice(0, line.shape[2])))
        elif kind == "rim":
            for c in (0, 1):
                first = tiles * deep + c * (2 * tiles + rows // 2) + 2 * tiles
                halos.append((k, owner, first, slice(c * (b - a), (c + 1) * (b - a))))
    copies = [pltpu.make_async_copy(src, dst, sem.at[m]) for m, (src, dst) in enumerate(copies)]
    lines = []
    for m, (k, owner, _, _) in enumerate(halos):
        at = jnp.where(flip == 0, jnp.minimum((owner + 1) * tiles, n * tiles - 1),
                       jnp.maximum(owner * tiles - 1, 0))
        at = pl.ds(pl.multiple_of(at * LANES, LANES), LANES)
        lines.append(pltpu.make_async_copy(field.at[:, :, at], line.at[m], line_sem.at[m]))
        lines[-1].start()
    for c in copies:
        c.start()
    stores = []
    for m, (k, owner, first, modes) in enumerate(halos):
        lines[m].wait()
        low = lax.broadcasted_iota(jnp.int32, line.shape[2:], 1) < NZ
        none = jnp.where(flip == 0, owner == n - 1, owner == 0)
        for i in range(rows // 2):
            one, two = line[m, 2 * i].astype(F32), line[m, 2 * i + 1].astype(F32)
            front = jnp.where(low, one, pltpu.roll(two, NZ, 1))
            back = jnp.where(low, pltpu.roll(one, NZ, 1), two)
            value = jnp.where(flip == 0, front, back)
            packed[m, i] = jnp.where(none, 0.0, value).astype(BF)
        stores.append(
            pltpu.make_async_copy(
                packed.at[m, :, modes], outs[k].at[first : first + rows // 2], out_sem.at[m]
            )
        )
        stores[-1].start()
    for c in copies + stores:
        c.wait()


def pack(jobs, n, tiles, order, field):
    rows, count, _ = field.shape
    shapes, pieces, lines = [], 0, 0
    for d, kind, a, b in jobs:
        if kind == "full":
            shapes.append((tiles * rows + rows // 2, count, LANES))
            pieces += tiles
            lines += 1
        elif kind == "rim":
            shapes.append((tiles * (rows - 2) + 2 * (tiles * 2 + rows // 2), b - a, LANES))
            pieces += 5 * tiles
            lines += 2
        else:
            shapes.append((tiles * (rows - 2), b - a, LANES))
            pieces += tiles
    anywhere = pl.BlockSpec(memory_space=pltpu.HBM)
    lines = max(lines, 1)
    return pl.pallas_call(
        functools.partial(pack_kernel, jobs, n, rows, tiles),
        in_specs=[pl.BlockSpec(memory_space=pltpu.SMEM), anywhere],
        out_specs=[anywhere] * len(jobs),
        out_shape=[jax.ShapeDtypeStruct(s, BF) for s in shapes],
        scratch_shapes=[
            VMEM((lines, rows, count, LANES), BF),
            VMEM((lines, rows // 2, count, LANES), BF),
            pltpu.SemaphoreType.DMA((pieces,)),
            pltpu.SemaphoreType.DMA((lines,)),
            pltpu.SemaphoreType.DMA((lines,)),
        ],
        compiler_params=pltpu.CompilerParams(vmem_limit_bytes=16 << 20),
    )(order, field)


def spread_out(total, n, space, q, count):
    share = n * count // space
    out = []
    for s in range(space):
        start = ((s * share) // count ^ q) * count + (s * share) % count
        rows = lax.dynamic_slice_in_dim(total, start, share, axis=0)
        out += [lax.dynamic_slice_in_dim(rows, (z ^ q) * count, count, axis=1) for z in range(n)]
    return jnp.stack(out)


def after(value, token):
    return lax.optimization_barrier((value, token))[0]


def local(modes, phases, velocity):
    space, n = lax.axis_size("space"), lax.axis_size("mode")
    sp, q = lax.axis_index("space"), lax.axis_index("mode")
    count, rows, plane = modes.shape
    width = plane // n
    tiles = width // LANES
    eps = 1.0 / math.sqrt(space * rows * plane)
    field = jnp.transpose(modes, (1, 0, 2))
    flip = sp & 1

    weight = jnp.where(phases == 0, 0.1, jnp.where(phases == 1, 1.0, 0.5)).astype(F32)
    w = lax.dynamic_slice_in_dim(weight, q * width, width, axis=1)[:, None, :]

    def line_start(owner):
        end = jnp.minimum((owner + 1) * width, plane - NZ)
        return jnp.where(flip == 0, end, jnp.maximum(owner * width - NZ, 0))

    wh = lax.dynamic_slice_in_dim(weight, line_start(q), NZ, axis=1).reshape(rows // 2, 1, LANES)

    def slab(source, owner):
        return lax.dynamic_slice_in_dim(source, owner * width, width, axis=2)

    def line(source, owner):
        part = lax.dynamic_slice_in_dim(source, line_start(owner), NZ, axis=2)
        none = jnp.where(flip == 0, owner == n - 1, owner == 0)
        part = jnp.where(none, jnp.zeros_like(part), part)
        return jnp.concatenate([part[0::2], part[1::2]], axis=-1)

    up = [(i, i + 1) for i in range(space - 1)]
    down = [(i + 1, i) for i in range(space - 1)]

    def edges(first, last):
        return lax.ppermute(last, "space", up), lax.ppermute(first, "space", down)

    def swap(part, d):
        return lax.ppermute(part, "mode", [(i, i ^ d) for i in range(n)])

    order = jnp.stack([q, flip])
    base = dict(rows=rows, tiles=tiles, eps=eps, n=n, space=space, last=False, off=0, d=0, vmem=16, edge=0)
    if n != 4:
        xs, hs = [slab(field, q)], [line(field, q)]
        for d in range(1, n):
            xs.append(swap(slab(field, q ^ d), d))
            hs.append(swap(line(field, q ^ d), d))
        x, h = jnp.concatenate(xs, axis=1), jnp.concatenate(hs, axis=1)
        cfg = dict(base, whole=n * count, count=n * count, n_blocks=1, old=[], vmem=40)
        xd, xu = edges(x[:1], x[rows - 1 :])
        x = jnp.concatenate([x, h], axis=0)
        _, total = phase(cfg, order, velocity, w, wh, xd, xu, [x], [], None, None)
        tiles = spread_out(total, n, space, q, count)
    else:
        half = count // 2
        p3, p1 = pack([(3, "full", 0, 0), (1, "full", 0, 0)], n, tiles, order, field)
        x3, x1 = swap(p3, 3), swap(p1, 1)
        jobs = [(2, "rim", 0, half), (2, "inner", half, count), (0, "full", 0, 0)]
        p2, p2b, x0 = pack(jobs, n, tiles, order, after(field, p1))
        front, back = swap(p2, 2), swap(p2b, 2)
        pick = lambda x, r: [x[t * rows + r][None] for t in range(tiles)]
        join = lambda pieces: jnp.concatenate(pieces, axis=0)
        base = dict(base, whole=count, n_blocks=n)
        full = dict(base, count=count)
        xd, xu = edges(join(pick(x0, 0)), join(pick(x0, rows - 1)))
        kept, g = phase(dict(full, old=[]), order, velocity, w, wh, xd, xu, [x0], [], None, None)
        names, old = [0], [kept]
        x3 = after(x3, g)
        xd, xu = edges(
            join(pick(x3, 0) + pick(x1, 0)), join(pick(x3, rows - 1) + pick(x1, rows - 1))
        )
        for k, (d, x) in enumerate(((3, x3), (1, x1))):
            cfg = dict(full, d=d, old=list(names), edge=k * tiles)
            kept, g = phase(cfg, order, velocity, w, wh, xd, xu, [x], old, None, g)
            names, old = [*names, d], [*old, kept]
        front = after(front, g)
        start, step = tiles * (rows - 2), 2 * tiles + rows // 2
        rims = [front[start + c * step : start + c * step + 2 * tiles] for c in (0, 1)]
        xd, xu = edges(join([r[::2] for r in rims]), join([r[1::2] for r in rims]))
        part = dict(base, d=2, count=half, old=names)
        kept, g = phase(part, order, velocity, w, wh, xd, xu, [front], old, None, g)
        back = after(back, g)
        part = dict(part, off=half, edge=tiles, last=True)
        _, g = phase(part, order, velocity, w, wh, xd, xu, [front, back], old, kept, g)
        tiles = g
    arrived = lax.all_to_all(tiles, ("space", "mode"), split_axis=0, concat_axis=0, tiled=True)
    return jnp.sum(arrived.astype(F32), axis=0) * eps


def solution(mesh):
    placed = (P("mode", "space", None), P("space", None), P())
    return jax.shard_map(
        local, mesh=mesh, in_specs=placed, out_specs=P("space", "mode"), check_vma=False
    )
```

```python
import functools
import math

import jax
import jax.numpy as jnp
from jax import lax
from jax.experimental import pallas as pl
from jax.experimental.pallas import tpu as pltpu
from jax.sharding import PartitionSpec as P

NZ = 64
LANES = 128
SUB = 16
PACK_VMEM = 16
BF = jnp.bfloat16
F32 = jnp.float32
VMEM = pltpu.VMEM


def product(left, right):
    return lax.dot_general(left, right, (((1,), (1,)), ((), ())), preferred_element_type=F32)


def apply_rows(i, eps, velocity, w, xs, a, tiles, rows, off, count):
    span = rows + 2
    xp, xm = eps - 0.5 * velocity[0], eps + 0.5 * velocity[0]
    yp, ym = eps - 0.5 * velocity[1], eps + 0.5 * velocity[1]
    zp, zm = eps - 0.5 * velocity[2], eps + 0.5 * velocity[2]
    lane = lax.broadcasted_iota(jnp.int32, (SUB, LANES), 1)
    low = lane < NZ
    zps = jnp.where(lane % NZ == NZ - 1, 0.0, zp)
    zms = jnp.where(lane % NZ == 0, 0.0, zm)
    own = jnp.where(low, yp, ym)
    other = jnp.where(low, ym, yp)

    def body(j, carry):
        source = pl.ds(pl.multiple_of(j * SUB, SUB), SUB)
        target = pl.ds(pl.multiple_of(j * SUB + off, SUB), SUB)
        center = [
            [xs[t * span + 2 * i + r, source, :].astype(F32) for t in range(tiles)] for r in range(4)
        ]
        for r in (0, 1):
            mid = center[r + 1]
            turned = [pltpu.roll(c, NZ, 1) for c in mid]
            for t in range(tiles):
                c = mid[t]
                behind = turned[t + 1] if t + 1 < tiles else jnp.zeros_like(c)
                before = turned[t - 1] if t > 0 else jnp.zeros_like(c)
                value = xp * center[r + 2][t] + xm * center[r][t]
                value = value + own * turned[t] + other * jnp.where(low, before, behind)
                value = value + zps * pltpu.roll(c, LANES - 1, 1) + zms * pltpu.roll(c, 1, 1)
                value = (value - (6.0 * eps) * c) * w[2 * i + r, :, t * LANES : (t + 1) * LANES]
                a[t * rows + 2 * i + r, target, :] = value.astype(BF)
        return carry

    lax.fori_loop(0, count // SUB, body, 0)


def phase_kernel(cfg, *refs):
    refs = list(refs)
    d, off, count, whole = cfg["d"], cfg["off"], cfg["count"], cfg["whole"]
    rows, tiles = cfg["rows"], cfg["tiles"]
    steps, end, mine, span = rows // 2, off + count, slice(off, off + count), rows + 2
    last, part = cfg["last"], count < whole
    take = lambda k: [refs.pop(0) for _ in range(k)]
    order, velocity, w = take(3)
    parts = take(cfg["n_parts"])
    old = [take(2) for _ in range(cfg["n_old"])]
    prev = take(2) if cfg["prev"] else None
    gin = take(1)[0] if cfg["gin"] else None
    xo = take(1)[0] if part and not last else None
    a = None if last else take(1)[0]
    (gout,) = take(1)
    if last:
        (a,) = take(1)
    xs, t2 = take(2)
    t1 = take(1)[0] if cfg["t1"] else None
    g = gout
    loads = []
    if old or prev is not None:
        held, sem = take(2)
        sources = [v for pair in old for v in pair] + list(prev or [])
        for k, v in enumerate(sources):
            loads.append(pltpu.make_async_copy(v, held.at[k], sem.at[k]))
            loads[-1].start()
        old = [(held.at[2 * k], held.at[2 * k + 1]) for k in range(len(old))]
        if prev is not None:
            prev = (held.at[2 * len(old)], held.at[2 * len(old) + 1])

    if part:
        rim, inner = parts[0], parts[-1]
        deep = rows - 2
        begin = inner.shape[0] - (tiles - 2) * deep
        base = (off // count) * (2 * tiles + 2 * deep)
        sides = (base + 2 * tiles, base + 2 * tiles + deep)
    for t in range(tiles):
        xs[t * span] = jnp.zeros_like(xs[0])
        xs[t * span + rows + 1] = jnp.zeros_like(xs[0])
        if part:
            xs[t * span + 1] = rim[base + t]
            xs[t * span + rows] = rim[base + tiles + t]
            if t in (0, tiles - 1):
                first = sides[t // (tiles - 1)]
                xs[t * span + 2 : t * span + rows] = rim[first : first + deep]
            else:
                xs[t * span + 2 : t * span + rows] = inner[begin + (t - 1) * deep : begin + t * deep]
        else:
            xs[t * span + 1 : t * span + rows + 1] = parts[0][t * rows : (t + 1) * rows]
    t2[...] = jnp.zeros_like(t2)
    if t1 is not None:
        t1[...] = jnp.zeros_like(t1)
    def padded(value, before=None):
        pieces = [value]
        if off:
            pieces.insert(0, jnp.zeros((off, LANES), BF) if before is None else before)
        if end < whole:
            pieces.append(jnp.zeros((whole - end, LANES), BF))
        return pieces[0] if len(pieces) == 1 else jnp.concatenate(pieces, axis=0)

    def stencil(i, carry):
        apply_rows(i, cfg["eps"], velocity, w, xs, a, tiles, rows, off, count)
        return carry

    lax.fori_loop(0, steps, stencil, 0)
    for c in loads:
        c.wait()

    def body(i, carry):
        picks = [t * rows + 2 * i + r for r in (0, 1) for t in range(tiles)]
        wide = lambda ref: jnp.concatenate([ref[k] for k in picks], axis=1)
        new = [xs[t * span + 2 * i + r + 1] for r in (0, 1) for t in range(tiles)]
        if part:
            before = [None if prev is None else prev[0][k, :off, :] for k in picks]
            both = [padded(v, u) for v, u in zip(new, before)]
            if xo is not None:
                for k, v in zip(picks, both):
                    xo[k] = v
        else:
            both = new
        fresh = [padded(v) for v in new]
        mark = [padded(a[k, mine, :]) for k in picks]
        if part and not last:
            rest = slice(0, off) if off else slice(end, whole)
            for k in picks:
                a[k, rest, :] = jnp.zeros((whole - count, LANES), BF) if prev is None else prev[1][k, rest, :]
        tall = [wide(ox) for ox, _ in old] + [jnp.concatenate(both, axis=1)]
        t2[...] += product(jnp.concatenate(tall, axis=0), jnp.concatenate(mark, axis=1))
        tall = [wide(oa) for _, oa in old] + ([wide(prev[1])] if prev is not None else [])
        if tall:
            t1[...] += product(jnp.concatenate(tall, axis=0), jnp.concatenate(fresh, axis=1))
        return carry

    lax.fori_loop(0, steps, body, 0)

    g[...] = jnp.zeros_like(g) if gin is None else gin[...]
    block = lambda k: slice(k * whole, (k + 1) * whole)
    names = [*cfg["old"], d]
    for k, o in enumerate(names):
        g[block(o), block(d)] += t2[block(k), :]
    for k, o in enumerate(names if prev is not None else names[:-1]):
        g[block(d), block(o)] += t1[block(k), :].T


def phase(cfg, order, velocity, w, parts, old, prev, gin):
    rows, tiles, whole, count = cfg["rows"], cfg["tiles"], cfg["whole"], cfg["count"]
    size, last, part = cfg["n_blocks"] * whole, cfg["last"], count < whole
    kept = jax.ShapeDtypeStruct((tiles * rows, whole, LANES), BF)
    args = [order, velocity, w, *parts]
    first = len(args)
    for group in [*old, *([prev] if prev is not None else [])]:
        args += list(group)
    loaded = len(args) - first
    if gin is not None:
        args.append(gin)
    scratch = []
    if last:
        out_shape = []
        scratch.append(VMEM(kept.shape, BF))
    else:
        out_shape = [kept] * (2 if part else 1)
    out_shape.append(jax.ShapeDtypeStruct((size, size), F32))
    seconds = len(old) + (prev is not None)
    scratch.append(VMEM((tiles * (rows + 2), count, LANES), BF))
    scratch.append(VMEM(((len(old) + 1) * whole, whole), F32))
    if seconds:
        scratch.append(VMEM((seconds * whole, whole), F32))
    if loaded:
        scratch += [VMEM((loaded, *kept.shape), BF), pltpu.SemaphoreType.DMA((loaded,))]
    elements = rows * count * tiles * LANES
    cfg = dict(cfg, n_parts=len(parts), n_old=len(old), prev=prev is not None, gin=gin is not None, t1=bool(seconds))
    vmem = pl.BlockSpec(memory_space=VMEM)
    smem = pl.BlockSpec(memory_space=pltpu.SMEM)
    outs = pl.pallas_call(
        functools.partial(phase_kernel, cfg),
        in_specs=[smem, smem]
        + [pl.BlockSpec(memory_space=pl.ANY) if first <= k < first + loaded else vmem for k in range(2, len(args))],
        out_specs=[vmem] * len(out_shape),
        out_shape=out_shape,
        scratch_shapes=scratch,
        compiler_params=pltpu.CompilerParams(vmem_limit_bytes=cfg["vmem"] << 20),
        cost_estimate=pl.CostEstimate(flops=1, bytes_accessed=1, transcendentals=0),
    )(*args)
    if last:
        return None, outs[0]
    return (outs[0] if part else parts[0], outs[-2]), outs[-1]


def line_kernel(rows, tiles, flip, *refs):
    ins, (near, far, near_row, far_row) = refs[:-4], refs[-4:]
    deep = rows - 2

    def tile_row(ref, row, t, c):
        if c is None:
            return ref[t * rows + row].astype(F32)
        base = c * (2 * tiles + 2 * deep)
        if row in (0, rows - 1):
            return ref[base + (tiles if row else 0) + t].astype(F32)
        return ref[base + 2 * tiles + (deep if t else 0) + row - 1].astype(F32)

    parts = []
    for ref in ins:
        parts += [(ref, None)] if ref.shape[0] == tiles * rows else [(ref, 0), (ref, 1)]
    keep = flip[0] == 0
    start = 0
    for ref, c in parts:
        size = ref.shape[1]
        low = lax.broadcasted_iota(jnp.int32, (size, LANES), 1) < NZ
        modes = slice(start, start + size)
        start += size
        for t in range(tiles):
            near_row[t, modes, :] = tile_row(ref, 0, t, c).astype(BF)
            far_row[t, modes, :] = tile_row(ref, rows - 1, t, c).astype(BF)
        for i in range(rows // 2):
            one, two = tile_row(ref, 2 * i, 0, c), tile_row(ref, 2 * i + 1, 0, c)
            first = jnp.where(low, one, pltpu.roll(two, NZ, 1))
            one, two = tile_row(ref, 2 * i, tiles - 1, c), tile_row(ref, 2 * i + 1, tiles - 1, c)
            final = jnp.where(low, pltpu.roll(one, NZ, 1), two)
            near[i, modes, :] = jnp.where(keep, first, final).astype(BF)
            far[i, modes, :] = jnp.where(keep, final, first).astype(BF)


def lines_of(arrays, rows, tiles, flip):
    modes = sum(v.shape[1] * (1 if v.shape[0] == tiles * rows else 2) for v in arrays)
    vmem = pl.BlockSpec(memory_space=VMEM)
    shape = jax.ShapeDtypeStruct((rows // 2, modes, LANES), BF)
    return pl.pallas_call(
        functools.partial(line_kernel, rows, tiles),
        in_specs=[pl.BlockSpec(memory_space=pltpu.SMEM)] + [vmem] * len(arrays),
        out_specs=[vmem] * 4,
        out_shape=[shape] * 2 + [jax.ShapeDtypeStruct((tiles, modes, LANES), BF)] * 2,
        compiler_params=pltpu.CompilerParams(vmem_limit_bytes=12 << 20),
        cost_estimate=pl.CostEstimate(flops=1, bytes_accessed=1, transcendentals=0),
    )(flip.reshape(1), *arrays)


def border_kernel(eps, groups, space, n, order, velocity, wn, wh, wr, wx, gin, *refs):
    count = len(groups)
    here, there = refs[:count], refs[count : 2 * count]
    own, over = refs[2 * count : 3 * count], refs[3 * count : 4 * count]
    g, out = refs[-1], refs[4 * count]
    xp, xm = eps - 0.5 * velocity[0], eps + 0.5 * velocity[0]
    yp, ym = eps - 0.5 * velocity[1], eps + 0.5 * velocity[1]
    toward = jnp.where(order[1] == 0, yp, ym)
    back = jnp.where(order[1] == 0, ym, yp)
    blocks = sum(len(names) for names in groups)
    size = g.shape[0] // blocks

    def find(refs, d, i):
        for names, ref in zip(groups, refs):
            if d in names:
                k = names.index(d)
                return ref[i, k * size : (k + 1) * size, :]

    def every(refs, i):
        return jnp.concatenate([find(refs, d, i) for d in range(blocks)], axis=0)

    left, right = [], []
    for k in range(wn.shape[0]):
        mine = every(here, k)
        if blocks == 4:
            near = order[2] == 1
            other = [
                jnp.where(near, find(there, d ^ 1, k).astype(F32), find(there, d ^ 3, k).astype(F32))
                for d in range(blocks)
            ]
            other = jnp.concatenate(other, axis=0)
        else:
            other = every(there, k).astype(F32)
        left += [mine, other.astype(BF)]
        right += [(wn[k] * (toward * other)).astype(BF), (wh[k] * (back * mine.astype(F32))).astype(BF)]
    for t in range(wr.shape[0]):
        mine, other = every(own, t), every(over, t)
        left += [mine, other]
        right += [
            (wr[t] * (xp * other.astype(F32))).astype(BF),
            (wx[t] * (xm * mine.astype(F32))).astype(BF),
        ]
    total = gin[...]
    for k in range(0, len(left), 4):
        total = total + product(
            jnp.concatenate(left[k : k + 4], axis=1), jnp.concatenate(right[k : k + 4], axis=1)
        )
    g[...] = total
    if blocks == n:
        q = order[0]
        share = out.shape[1]
        per = size // share
        for s in range(space):
            first = pl.multiple_of(((s // per) ^ q) * size + (s % per) * share, share)
            for z in range(n):
                start = pl.multiple_of((z ^ q) * size, size)
                out[s * n + z] = g[pl.ds(first, share), pl.ds(start, size)].astype(out.dtype)
    else:
        out[...] = total


def border(eps, groups, order, velocity, weights, gin, here, there, own, over, space, n):
    vmem = pl.BlockSpec(memory_space=VMEM)
    smem = pl.BlockSpec(memory_space=pltpu.SMEM)
    blocks = sum(len(names) for names in groups)
    shape = jax.ShapeDtypeStruct(gin.shape, F32)
    if blocks == n:
        size = gin.shape[0]
        shape = jax.ShapeDtypeStruct((space * n, size // space, size // n), BF)
    args = [order, velocity, *weights, gin, *here, *there, *own, *over]
    return pl.pallas_call(
        functools.partial(border_kernel, eps, groups, space, n),
        in_specs=[smem, smem] + [vmem] * (len(args) - 2),
        out_specs=vmem,
        out_shape=shape,
        scratch_shapes=[VMEM(gin.shape, F32)],
        compiler_params=pltpu.CompilerParams(vmem_limit_bytes=16 << 20),
        cost_estimate=pl.CostEstimate(flops=1, bytes_accessed=1, transcendentals=0),
    )(*args)


def pack_kernel(jobs, rows, tiles, order, field, *refs):
    outs, sem = refs[:-1], refs[-1]
    q = order[0]
    deep = rows - 2
    copies = []
    for k, (d, kind, a, b) in enumerate(jobs):
        base = (q ^ d) * tiles * LANES
        cut = lambda t: pl.ds(pl.multiple_of(base + t * LANES, LANES), LANES)
        for t in range(tiles):
            if kind == "full":
                copies.append((field.at[:, :, cut(t)], outs[k].at[t * rows : (t + 1) * rows]))
                continue
            inside = slice(1, rows - 1)
            if t not in (0, tiles - 1):
                begin = 2 * (2 * tiles + 2 * deep) if kind == "rim" else 0
                to = slice(begin + (t - 1) * deep, begin + t * deep)
                copies.append((field.at[inside, a:b, cut(t)], outs[k].at[to]))
            if kind == "rim":
                for c in (0, 1):
                    first = c * (2 * tiles + 2 * deep)
                    half = slice(c * (b - a), (c + 1) * (b - a))
                    copies.append((field.at[0, half, cut(t)], outs[k].at[first + t]))
                    copies.append((field.at[rows - 1, half, cut(t)], outs[k].at[first + tiles + t]))
                    if t in (0, tiles - 1):
                        to = first + 2 * tiles + (deep if t else 0)
                        copies.append((field.at[inside, half, cut(t)], outs[k].at[to : to + deep]))
    copies = [pltpu.make_async_copy(src, dst, sem.at[m]) for m, (src, dst) in enumerate(copies)]
    for c in copies:
        c.start()
    for c in copies:
        c.wait()


def pack(jobs, tiles, order, field):
    rows, count, _ = field.shape
    deep = rows - 2
    shapes, pieces = [], 0
    for d, kind, a, b in jobs:
        if kind == "full":
            shapes.append((tiles * rows, count, LANES))
            pieces += tiles
        else:
            length = (tiles - 2) * deep
            pieces += tiles - 2
            if kind == "rim":
                length += 2 * (2 * tiles + 2 * deep)
                pieces += 4 * tiles + 4
            shapes.append((length, b - a, LANES))
    anywhere = pl.BlockSpec(memory_space=pl.ANY)
    return pl.pallas_call(
        functools.partial(pack_kernel, jobs, rows, tiles),
        in_specs=[pl.BlockSpec(memory_space=pltpu.SMEM), anywhere],
        out_specs=[anywhere] * len(jobs),
        out_shape=[jax.ShapeDtypeStruct(s, BF) for s in shapes],
        scratch_shapes=[pltpu.SemaphoreType.DMA((pieces,))],
        compiler_params=pltpu.CompilerParams(vmem_limit_bytes=PACK_VMEM << 20),
    )(order, field)


def first_kernel(owners, rows, tiles, order, field, *refs):
    count = len(owners)
    outs, (stage, into, out_of) = refs[:count], refs[count:]
    loads, stores = [], []
    for k, d in enumerate(owners):
        wide = pl.ds(pl.multiple_of((order[0] ^ d) * tiles * LANES, LANES), tiles * LANES)
        loads.append(pltpu.make_async_copy(field.at[:, :, wide], stage.at[k], into.at[k]))
        loads[-1].start()
    for k in range(count):
        loads[k].wait()
        for t in range(tiles):
            lanes = slice(t * LANES, (t + 1) * LANES)
            to = outs[k].at[t * rows : (t + 1) * rows]
            stores.append(
                pltpu.make_async_copy(stage.at[k, :, :, lanes], to, out_of.at[k * tiles + t])
            )
            stores[-1].start()
    for c in stores:
        c.wait()


def first_pack(owners, tiles, order, field):
    rows, count, _ = field.shape
    shape = jax.ShapeDtypeStruct((tiles * rows, count, LANES), BF)
    anywhere = pl.BlockSpec(memory_space=pl.ANY)
    return pl.pallas_call(
        functools.partial(first_kernel, owners, rows, tiles),
        in_specs=[pl.BlockSpec(memory_space=pltpu.SMEM), anywhere],
        out_specs=[anywhere] * len(owners),
        out_shape=[shape] * len(owners),
        scratch_shapes=[
            VMEM((len(owners), rows, count, tiles * LANES), BF),
            pltpu.SemaphoreType.DMA((len(owners),)),
            pltpu.SemaphoreType.DMA((len(owners) * tiles,)),
        ],
        compiler_params=pltpu.CompilerParams(vmem_limit_bytes=60 << 20),
    )(order, field)


def spread_out(total, n, space, q, count):
    share = n * count // space
    out = []
    for s in range(space):
        start = ((s * share) // count ^ q) * count + (s * share) % count
        rows = lax.dynamic_slice_in_dim(total, start, share, axis=0)
        out += [lax.dynamic_slice_in_dim(rows, (z ^ q) * count, count, axis=1) for z in range(n)]
    return jnp.stack(out)


def after(value, token):
    return lax.optimization_barrier((value, token))[0]


def local(modes, phases, velocity):
    space, n = lax.axis_size("space"), lax.axis_size("mode")
    sp, q = lax.axis_index("space"), lax.axis_index("mode")
    count, rows, plane = modes.shape
    width = plane // n
    tiles = width // LANES
    eps = 1.0 / math.sqrt(space * rows * plane)
    field = jnp.transpose(modes, (1, 0, 2))
    flip = sp & 1

    weight = jnp.where(phases == 0, 0.1, jnp.where(phases == 1, 1.0, 0.5)).astype(F32)
    w = lax.dynamic_slice_in_dim(weight, q * width, width, axis=1)[:, None, :]

    near = jnp.where(flip == 0, jnp.minimum((q + 1) * width, plane - NZ), jnp.maximum(q * width - NZ, 0))
    mine = jnp.where(flip == 0, (q + 1) * width - NZ, q * width)
    wh, wn = [
        lax.dynamic_slice_in_dim(weight, v, NZ, axis=1).reshape(rows // 2, 1, LANES)
        for v in (near, mine)
    ]

    def slab(source, owner):
        return lax.dynamic_slice_in_dim(source, owner * width, width, axis=2)

    ahead = [(i + 1, i) for i in range(space - 1)]
    above = lambda v: lax.ppermute(v, "space", ahead)
    cut = lambda v: lax.dynamic_slice_in_dim(v, q * width, width, axis=1).reshape(tiles, 1, LANES)
    weights = (wn, wh, cut(weight[rows - 1 :]), cut(above(weight[:1])))

    def swap(part, d):
        return lax.ppermute(part, "mode", [(i, i ^ d) for i in range(n)])

    relay = [(s * n + i, s * n + i - 1 + 2 * (s & 1)) for s in range(space) for i in range(n)]
    relay = [(i, j) for i, j in relay if i // n == j // n and j >= 0]
    beside = lambda v: lax.ppermute(v, ("space", "mode"), relay)
    partner = jnp.clip(q + 1 - 2 * flip, 0, n - 1) ^ q
    order = jnp.stack([q, flip, partner])
    base = dict(rows=rows, tiles=tiles, eps=eps, n=n, space=space, last=False, off=0, d=0, vmem=24)
    if n != 4:
        xs = [slab(field, q)] + [swap(slab(field, q ^ d), d) for d in range(1, n)]
        x = jnp.concatenate(xs, axis=1)
        cfg = dict(base, whole=n * count, count=n * count, n_blocks=1, old=[], vmem=40)
        x = jnp.concatenate([x[:, :, t * LANES : (t + 1) * LANES] for t in range(tiles)], axis=0)
        _, total = phase(cfg, order, velocity, w, [x], [], None, None)
        send, here, send_row, own = lines_of([x], rows, tiles, flip)
        there = beside(send).reshape(rows // 2, n, count, LANES)
        there = there[:, jnp.arange(n) ^ partner].reshape(send.shape)
        total = border(eps, [[0]], order, velocity, weights, total, [here], [there], [own], [above(send_row)], space, n)
        tiles = spread_out(total, n, space, q, count)
    else:
        half = count // 2
        p1, p3 = first_pack((1, 3), tiles, order, field)
        x1, x3 = swap(p1, 1), swap(p3, 3)
        jobs = [(0, "full", 0, 0), (2, "rim", 0, half), (2, "inner", half, count)]
        x0, p2, p2b = pack(jobs, tiles, order, after(field, p3))
        front, back = swap(p2, 2), swap(p2b, 2)
        base = dict(base, whole=count, n_blocks=n)
        names, old, g, met = [], [], None, []

        def meet(*arrays):
            send, here, row, own = lines_of(arrays, rows, tiles, flip)
            met.append((here, beside(send), own, above(row)))

        x0 = after(x0, weights)
        for d, x in ((0, x0), (1, x1), (3, x3)):
            if names:
                x = after(x, g)
            if d == 3:
                meet(x0, x1, x)
            cfg = dict(base, count=count, d=d, old=list(names))
            kept, g = phase(cfg, order, velocity, w, [x], old, None, g)
            names, old = [*names, d], [*old, kept]
        front = after(front, (g, met[-1][3]))
        meet(front)
        part = dict(base, d=2, count=half, old=names)
        kept, g = phase(part, order, velocity, w, [front], old, None, g)
        back = after(back, (g, met[-1][3]))
        part = dict(part, off=half, last=True)
        _, g = phase(part, order, velocity, w, [front, back], old, kept, g)
        met = [list(v) for v in zip(*met)]
        g = border(eps, [[0, 1, 3], [2]], order, velocity, weights, g, *met, space, n)
        tiles = g
    arrived = lax.all_to_all(tiles, ("space", "mode"), split_axis=0, concat_axis=0, tiled=True)
    return jnp.sum(arrived.astype(F32), axis=0) * eps


def solution(mesh):
    placed = (P("mode", "space", None), P("space", None), P())
    return jax.shard_map(
        local, mesh=mesh, in_specs=placed, out_specs=P("space", "mode"), check_vma=False
    )
```

```python
import functools
import math

import jax
import jax.numpy as jnp
from jax import lax
from jax.experimental import pallas as pl
from jax.experimental.pallas import tpu as pltpu
from jax.sharding import PartitionSpec as P

NZ = 64
LANES = 128
SUB = 16
PACK_VMEM = 16
BF = jnp.bfloat16
F32 = jnp.float32
VMEM = pltpu.VMEM


def product(left, right):
    return lax.dot_general(left, right, (((1,), (1,)), ((), ())), preferred_element_type=F32)


def apply_rows(i, eps, velocity, w, xs, a, tiles, rows, off, count):
    span = rows + 2
    xp, xm = eps - 0.5 * velocity[0], eps + 0.5 * velocity[0]
    yp, ym = eps - 0.5 * velocity[1], eps + 0.5 * velocity[1]
    zp, zm = eps - 0.5 * velocity[2], eps + 0.5 * velocity[2]
    lane = lax.broadcasted_iota(jnp.int32, (SUB, LANES), 1)
    low = lane < NZ
    zps = jnp.where(lane % NZ == NZ - 1, 0.0, zp)
    zms = jnp.where(lane % NZ == 0, 0.0, zm)
    own = jnp.where(low, yp, ym)
    other = jnp.where(low, ym, yp)

    def body(j, carry):
        source = pl.ds(pl.multiple_of(j * SUB, SUB), SUB)
        target = pl.ds(pl.multiple_of(j * SUB + off, SUB), SUB)
        center = [
            [xs[t * span + 2 * i + r, source, :].astype(F32) for t in range(tiles)] for r in range(4)
        ]
        for r in (0, 1):
            mid = center[r + 1]
            turned = [pltpu.roll(c, NZ, 1) for c in mid]
            for t in range(tiles):
                c = mid[t]
                behind = turned[t + 1] if t + 1 < tiles else jnp.zeros_like(c)
                before = turned[t - 1] if t > 0 else jnp.zeros_like(c)
                value = xp * center[r + 2][t] + xm * center[r][t]
                value = value + own * turned[t] + other * jnp.where(low, before, behind)
                value = value + zps * pltpu.roll(c, LANES - 1, 1) + zms * pltpu.roll(c, 1, 1)
                value = (value - (6.0 * eps) * c) * w[2 * i + r, :, t * LANES : (t + 1) * LANES]
                a[t * rows + 2 * i + r, target, :] = value.astype(BF)
        return carry

    lax.fori_loop(0, count // SUB, body, 0)


def phase_kernel(cfg, *refs):
    refs = list(refs)
    take = lambda k: [refs.pop(0) for _ in range(k)]
    d, count, whole, index = cfg["d"], cfg["count"], cfg["whole"], cfg["index"]
    rows, tiles = cfg["rows"], cfg["tiles"]
    steps, span = rows // 2, rows + 2
    order, velocity, w = take(3)
    parts = take(cfg["n_parts"])
    old = [take(2) for _ in range(cfg["n_old"])]
    prev = take(2) if index == 1 else None
    gin = take(1)[0] if cfg["gin"] else None
    xo = take(1)[0] if index == 0 else None
    a = take(1)[0] if index != 1 else None
    gout = take(1)[0] if index != 0 else None
    if index == 1:
        (a,) = take(1)
    xs = take(1)[0]
    t2 = take(1)[0] if index != 0 else None
    t1 = take(1)[0] if old and index != 0 else None

    if index is not None:
        rim, inner = parts[0], parts[-1]
        deep = rows - 2
        begin = inner.shape[0] - (tiles - 2) * deep
        base = index * (2 * tiles + 2 * deep)
        sides = (base + 2 * tiles, base + 2 * tiles + deep)
    for t in range(tiles):
        xs[t * span] = jnp.zeros_like(xs[0])
        xs[t * span + rows + 1] = jnp.zeros_like(xs[0])
        if index is not None:
            xs[t * span + 1] = rim[base + t]
            xs[t * span + rows] = rim[base + tiles + t]
            if t in (0, tiles - 1):
                first = sides[t // (tiles - 1)]
                xs[t * span + 2 : t * span + rows] = rim[first : first + deep]
            else:
                xs[t * span + 2 : t * span + rows] = inner[begin + (t - 1) * deep : begin + t * deep]
        else:
            xs[t * span + 1 : t * span + rows + 1] = parts[0][t * rows : (t + 1) * rows]

    def stencil(i, carry):
        apply_rows(i, cfg["eps"], velocity, w, xs, a, tiles, rows, 0, count)
        return carry

    lax.fori_loop(0, steps, stencil, 0)
    if index == 0:
        for t in range(tiles):
            xo[t * rows : (t + 1) * rows] = xs[t * span + 1 : t * span + rows + 1]
        return

    t2[...] = jnp.zeros_like(t2)
    if t1 is not None:
        t1[...] = jnp.zeros_like(t1)

    def body(i, carry):
        pairs = [(r, t) for r in (0, 1) for t in range(tiles)]
        picks = [t * rows + 2 * i + r for r, t in pairs]
        join = lambda pieces: jnp.concatenate(pieces, axis=1)
        wide = lambda ref: join([ref[k] for k in picks])
        new = join([xs[t * span + 2 * i + r + 1] for r, t in pairs])
        mark = wide(a)
        if prev is not None:
            new = jnp.concatenate([wide(prev[0]), new], axis=0)
            mark = jnp.concatenate([wide(prev[1]), mark], axis=0)
        t2[...] += product(jnp.concatenate([wide(ox) for ox, _ in old] + [new], axis=0), mark)
        if old:
            t1[...] += product(jnp.concatenate([wide(oa) for _, oa in old], axis=0), new)
        return carry

    lax.fori_loop(0, steps, body, 0)

    gout[...] = jnp.zeros_like(gout) if gin is None else gin[...]
    block = lambda k: slice(k * whole, (k + 1) * whole)
    for k, o in enumerate([*cfg["old"], d]):
        gout[block(o), block(d)] += t2[block(k), :]
        if o != d:
            gout[block(d), block(o)] += t1[block(k), :].T


def phase(cfg, order, velocity, w, parts, old, prev, gin):
    rows, tiles, whole, count = cfg["rows"], cfg["tiles"], cfg["whole"], cfg["count"]
    size, index = cfg["n_blocks"] * whole, cfg["index"]
    kept = jax.ShapeDtypeStruct((tiles * rows, count, LANES), BF)
    total = jax.ShapeDtypeStruct((size, size), F32)
    args = [order, velocity, w, *parts]
    for group in [*old, *([prev] if prev is not None else [])]:
        args += list(group)
    if gin is not None:
        args.append(gin)
    out_shape = {None: [kept, total], 0: [kept, kept], 1: [total]}[index]
    scratch = [VMEM(kept.shape, BF)] if index == 1 else []
    scratch.append(VMEM((tiles * (rows + 2), count, LANES), BF))
    if index != 0:
        scratch.append(VMEM(((len(old) + 1) * whole, whole), F32))
        if old:
            scratch.append(VMEM((len(old) * whole, whole), F32))
    cfg = dict(cfg, n_parts=len(parts), n_old=len(old), gin=gin is not None)
    vmem = pl.BlockSpec(memory_space=VMEM)
    smem = pl.BlockSpec(memory_space=pltpu.SMEM)
    return pl.pallas_call(
        functools.partial(phase_kernel, cfg),
        in_specs=[smem, smem] + [vmem] * (len(args) - 2),
        out_specs=[vmem] * len(out_shape),
        out_shape=out_shape,
        scratch_shapes=scratch,
        compiler_params=pltpu.CompilerParams(vmem_limit_bytes=cfg["vmem"] << 20),
        cost_estimate=pl.CostEstimate(flops=1, bytes_accessed=1, transcendentals=0),
    )(*args)


def line_kernel(rows, tiles, choice, order, *refs):
    ins, (near, far, near_row, far_row) = refs[:-4], refs[-4:]
    deep = rows - 2
    keep = order[1] == 0

    def tile_row(ref, row, t, c):
        if c is None:
            return ref[t * rows + row].astype(F32)
        base = c * (2 * tiles + 2 * deep)
        if row in (0, rows - 1):
            return ref[base + (tiles if row else 0) + t].astype(F32)
        return ref[base + 2 * tiles + (deep if t else 0) + row - 1].astype(F32)

    def parts_of(ref):
        return [(ref, None)] if ref.shape[0] == tiles * rows else [(ref, 0), (ref, 1)]

    def line(ref, c, i, first):
        t = 0 if first else tiles - 1
        low = lax.broadcasted_iota(jnp.int32, (ref.shape[1], LANES), 1) < NZ
        one, two = tile_row(ref, 2 * i, t, c), tile_row(ref, 2 * i + 1, t, c)
        if first:
            return jnp.where(low, one, pltpu.roll(two, NZ, 1))
        return jnp.where(low, pltpu.roll(one, NZ, 1), two)

    start = 0
    for ref in ins[: choice[2]]:
        for ref, c in parts_of(ref):
            modes = slice(start, start + ref.shape[1])
            start += ref.shape[1]
            for t in range(tiles):
                near_row[t, modes, :] = tile_row(ref, 0, t, c).astype(BF)
                far_row[t, modes, :] = tile_row(ref, rows - 1, t, c).astype(BF)
            for i in range(rows // 2):
                value = jnp.where(keep, line(ref, c, i, False), line(ref, c, i, True))
                far[i, modes, :] = value.astype(BF)

    def send(ref):
        start = 0
        for ref, c in parts_of(ref):
            modes = slice(start, start + ref.shape[1])
            start += ref.shape[1]
            for i in range(rows // 2):
                value = jnp.where(keep, line(ref, c, i, True), line(ref, c, i, False))
                near[i, modes, :] = value.astype(BF)

    if choice[0] == choice[1]:
        send(ins[choice[0]])
    else:
        pl.when(order[2] == 1)(lambda: send(ins[choice[0]]))
        pl.when(order[2] != 1)(lambda: send(ins[choice[1]]))


def lines_of(arrays, rows, tiles, order, choice):
    size = lambda v: v.shape[1] * (1 if v.shape[0] == tiles * rows else 2)
    modes = sum(size(v) for v in arrays[: choice[2]])
    vmem = pl.BlockSpec(memory_space=VMEM)
    lines = lambda m: jax.ShapeDtypeStruct((rows // 2, m, LANES), BF)
    row = jax.ShapeDtypeStruct((tiles, modes, LANES), BF)
    return pl.pallas_call(
        functools.partial(line_kernel, rows, tiles, choice),
        in_specs=[pl.BlockSpec(memory_space=pltpu.SMEM)] + [vmem] * len(arrays),
        out_specs=[vmem] * 4,
        out_shape=[lines(size(arrays[choice[0]])), lines(modes), row, row],
        compiler_params=pltpu.CompilerParams(vmem_limit_bytes=12 << 20),
        cost_estimate=pl.CostEstimate(flops=1, bytes_accessed=1, transcendentals=0),
    )(order, *arrays)


def halo_kernel(n, tiles, order, field, *refs):
    outs, (line, sem) = refs[:2], refs[2:]
    q, flip = order[0], order[1]
    copies = []
    for d in (0, 1):
        owner = q ^ d
        at = jnp.where(
            flip == 0,
            jnp.minimum((owner + 1) * tiles, n * tiles - 1),
            jnp.maximum(owner * tiles - 1, 0),
        )
        at = pl.ds(pl.multiple_of(at * LANES, LANES), LANES)
        copies.append(pltpu.make_async_copy(field.at[:, :, at], line.at[d], sem.at[d]))
        copies[-1].start()
    low = lax.broadcasted_iota(jnp.int32, line.shape[2:], 1) < NZ
    for d in (0, 1):
        copies[d].wait()
        owner = q ^ d
        none = jnp.where(flip == 0, owner == n - 1, owner == 0)
        for i in range(line.shape[1] // 2):
            one, two = line[d, 2 * i].astype(F32), line[d, 2 * i + 1].astype(F32)
            front = jnp.where(low, one, pltpu.roll(two, NZ, 1))
            back = jnp.where(low, pltpu.roll(one, NZ, 1), two)
            value = jnp.where(flip == 0, front, back)
            outs[d][i] = jnp.where(none, 0.0, value).astype(BF)


def halos_of(n, tiles, order, field):
    rows, count, _ = field.shape
    shape = jax.ShapeDtypeStruct((rows // 2, count, LANES), BF)
    return pl.pallas_call(
        functools.partial(halo_kernel, n, tiles),
        in_specs=[pl.BlockSpec(memory_space=pltpu.SMEM), pl.BlockSpec(memory_space=pl.ANY)],
        out_specs=[pl.BlockSpec(memory_space=VMEM)] * 2,
        out_shape=[shape] * 2,
        scratch_shapes=[VMEM((2, rows, count, LANES), BF), pltpu.SemaphoreType.DMA((2,))],
        compiler_params=pltpu.CompilerParams(vmem_limit_bytes=12 << 20),
        cost_estimate=pl.CostEstimate(flops=1, bytes_accessed=1, transcendentals=0),
    )(order, field)


def border_kernel(eps, groups, beyond, space, n, order, velocity, wn, wh, wr, wx, gin, *refs):
    count = len(groups)
    here, own, over = refs[:count], refs[count : 2 * count], refs[2 * count : 3 * count]
    there, (out, g) = refs[3 * count : -2], refs[-2:]
    xp, xm = eps - 0.5 * velocity[0], eps + 0.5 * velocity[0]
    yp, ym = eps - 0.5 * velocity[1], eps + 0.5 * velocity[1]
    toward = jnp.where(order[1] == 0, yp, ym)
    back = jnp.where(order[1] == 0, ym, yp)
    blocks = sum(len(names) for names in groups)
    size = g.shape[0] // blocks

    def find(refs, d, i, groups=groups):
        for names, ref in zip(groups, refs):
            if d in names:
                k = names.index(d)
                return ref[i, k * size : (k + 1) * size, :]

    def every(refs, i, groups=groups):
        return jnp.concatenate([find(refs, d, i, groups) for d in range(blocks)], axis=0)

    left, right = [], []
    for k in range(wn.shape[0]):
        mine = every(here, k)
        other = every(there, k, beyond).astype(F32)
        left += [mine, other.astype(BF)]
        right += [(wn[k] * (toward * other)).astype(BF), (wh[k] * (back * mine.astype(F32))).astype(BF)]
    for t in range(wr.shape[0]):
        mine, other = every(own, t), every(over, t)
        left += [mine, other]
        right += [
            (wr[t] * (xp * other.astype(F32))).astype(BF),
            (wx[t] * (xm * mine.astype(F32))).astype(BF),
        ]
    total = gin[...]
    for k in range(0, len(left), 4):
        total = total + product(
            jnp.concatenate(left[k : k + 4], axis=1), jnp.concatenate(right[k : k + 4], axis=1)
        )
    g[...] = total
    if blocks == n:
        q = order[0]
        share = out.shape[1]
        per = size // share
        for s in range(space):
            first = pl.multiple_of(((s // per) ^ q) * size + (s % per) * share, share)
            for z in range(n):
                start = pl.multiple_of((z ^ q) * size, size)
                out[s * n + z] = g[pl.ds(first, share), pl.ds(start, size)].astype(out.dtype)
    else:
        out[...] = total


def border(eps, groups, beyond, order, velocity, weights, gin, here, own, over, there, space, n):
    vmem = pl.BlockSpec(memory_space=VMEM)
    smem = pl.BlockSpec(memory_space=pltpu.SMEM)
    blocks = sum(len(names) for names in groups)
    shape = jax.ShapeDtypeStruct(gin.shape, F32)
    if blocks == n:
        size = gin.shape[0]
        shape = jax.ShapeDtypeStruct((space * n, size // space, size // n), BF)
    args = [order, velocity, *weights, gin, *here, *own, *over, *there]
    return pl.pallas_call(
        functools.partial(border_kernel, eps, groups, beyond, space, n),
        in_specs=[smem, smem] + [vmem] * (len(args) - 2),
        out_specs=vmem,
        out_shape=shape,
        scratch_shapes=[VMEM(gin.shape, F32)],
        compiler_params=pltpu.CompilerParams(vmem_limit_bytes=16 << 20),
        cost_estimate=pl.CostEstimate(flops=1, bytes_accessed=1, transcendentals=0),
    )(*args)


def pack_kernel(jobs, rows, tiles, order, field, *refs):
    outs, sem = refs[:-1], refs[-1]
    q = order[0]
    deep = rows - 2
    copies = []
    for k, (d, kind, a, b) in enumerate(jobs):
        base = (q ^ d) * tiles * LANES
        cut = lambda t: pl.ds(pl.multiple_of(base + t * LANES, LANES), LANES)
        for t in range(tiles):
            if kind == "full":
                copies.append((field.at[:, :, cut(t)], outs[k].at[t * rows : (t + 1) * rows]))
                continue
            inside = slice(1, rows - 1)
            if t not in (0, tiles - 1):
                begin = 2 * (2 * tiles + 2 * deep) if kind == "rim" else 0
                to = slice(begin + (t - 1) * deep, begin + t * deep)
                copies.append((field.at[inside, a:b, cut(t)], outs[k].at[to]))
            if kind == "rim":
                for c in (0, 1):
                    first = c * (2 * tiles + 2 * deep)
                    half = slice(c * (b - a), (c + 1) * (b - a))
                    copies.append((field.at[0, half, cut(t)], outs[k].at[first + t]))
                    copies.append((field.at[rows - 1, half, cut(t)], outs[k].at[first + tiles + t]))
                    if t in (0, tiles - 1):
                        to = first + 2 * tiles + (deep if t else 0)
                        copies.append((field.at[inside, half, cut(t)], outs[k].at[to : to + deep]))
    copies = [pltpu.make_async_copy(src, dst, sem.at[m]) for m, (src, dst) in enumerate(copies)]
    for c in copies:
        c.start()
    for c in copies:
        c.wait()


def pack(jobs, tiles, order, field):
    rows, count, _ = field.shape
    deep = rows - 2
    shapes, pieces = [], 0
    for d, kind, a, b in jobs:
        if kind == "full":
            shapes.append((tiles * rows, count, LANES))
            pieces += tiles
        else:
            length = (tiles - 2) * deep
            pieces += tiles - 2
            if kind == "rim":
                length += 2 * (2 * tiles + 2 * deep)
                pieces += 4 * tiles + 4
            shapes.append((length, b - a, LANES))
    anywhere = pl.BlockSpec(memory_space=pl.ANY)
    return pl.pallas_call(
        functools.partial(pack_kernel, jobs, rows, tiles),
        in_specs=[pl.BlockSpec(memory_space=pltpu.SMEM), anywhere],
        out_specs=[anywhere] * len(jobs),
        out_shape=[jax.ShapeDtypeStruct(s, BF) for s in shapes],
        scratch_shapes=[pltpu.SemaphoreType.DMA((pieces,))],
        compiler_params=pltpu.CompilerParams(vmem_limit_bytes=PACK_VMEM << 20),
    )(order, field)


def first_kernel(owners, rows, tiles, order, field, *refs):
    count = len(owners)
    outs, (stage, into, out_of) = refs[:count], refs[count:]
    loads, stores = [], []
    for k, d in enumerate(owners):
        wide = pl.ds(pl.multiple_of((order[0] ^ d) * tiles * LANES, LANES), tiles * LANES)
        loads.append(pltpu.make_async_copy(field.at[:, :, wide], stage.at[k], into.at[k]))
        loads[-1].start()
    for k in range(count):
        loads[k].wait()
        for t in range(tiles):
            lanes = slice(t * LANES, (t + 1) * LANES)
            to = outs[k].at[t * rows : (t + 1) * rows]
            stores.append(
                pltpu.make_async_copy(stage.at[k, :, :, lanes], to, out_of.at[k * tiles + t])
            )
            stores[-1].start()
    for c in stores:
        c.wait()


def first_pack(owners, tiles, order, field):
    rows, count, _ = field.shape
    shape = jax.ShapeDtypeStruct((tiles * rows, count, LANES), BF)
    anywhere = pl.BlockSpec(memory_space=pl.ANY)
    return pl.pallas_call(
        functools.partial(first_kernel, owners, rows, tiles),
        in_specs=[pl.BlockSpec(memory_space=pltpu.SMEM), anywhere],
        out_specs=[anywhere] * len(owners),
        out_shape=[shape] * len(owners),
        scratch_shapes=[
            VMEM((len(owners), rows, count, tiles * LANES), BF),
            pltpu.SemaphoreType.DMA((len(owners),)),
            pltpu.SemaphoreType.DMA((len(owners) * tiles,)),
        ],
        compiler_params=pltpu.CompilerParams(vmem_limit_bytes=60 << 20),
    )(order, field)


def spread_out(total, n, space, q, count):
    share = n * count // space
    out = []
    for s in range(space):
        start = ((s * share) // count ^ q) * count + (s * share) % count
        rows = lax.dynamic_slice_in_dim(total, start, share, axis=0)
        out += [lax.dynamic_slice_in_dim(rows, (z ^ q) * count, count, axis=1) for z in range(n)]
    return jnp.stack(out)


def after(value, token):
    return lax.optimization_barrier((value, token))[0]


def local(modes, phases, velocity):
    space, n = lax.axis_size("space"), lax.axis_size("mode")
    sp, q = lax.axis_index("space"), lax.axis_index("mode")
    count, rows, plane = modes.shape
    width = plane // n
    tiles = width // LANES
    eps = 1.0 / math.sqrt(space * rows * plane)
    field = jnp.transpose(modes, (1, 0, 2))
    flip = sp & 1

    weight = jnp.where(phases == 0, 0.1, jnp.where(phases == 1, 1.0, 0.5)).astype(F32)
    w = lax.dynamic_slice_in_dim(weight, q * width, width, axis=1)[:, None, :]

    near = jnp.where(flip == 0, jnp.minimum((q + 1) * width, plane - NZ), jnp.maximum(q * width - NZ, 0))
    mine = jnp.where(flip == 0, (q + 1) * width - NZ, q * width)
    wh, wn = [
        lax.dynamic_slice_in_dim(weight, v, NZ, axis=1).reshape(rows // 2, 1, LANES)
        for v in (near, mine)
    ]

    def slab(source, owner):
        return lax.dynamic_slice_in_dim(source, owner * width, width, axis=2)

    ahead = [(i + 1, i) for i in range(space - 1)]
    above = lambda v: lax.ppermute(v, "space", ahead)
    cut = lambda v: lax.dynamic_slice_in_dim(v, q * width, width, axis=1).reshape(tiles, 1, LANES)
    weights = (wn, wh, cut(weight[rows - 1 :]), cut(above(weight[:1])))

    def swap(part, d):
        return lax.ppermute(part, "mode", [(i, i ^ d) for i in range(n)])

    relay = [(s * n + i, s * n + i - 1 + 2 * (s & 1)) for s in range(space) for i in range(n)]
    relay = [(i, j) for i, j in relay if i // n == j // n and j >= 0]
    beside = lambda v: lax.ppermute(v, ("space", "mode"), relay)
    source = jnp.clip(q + 1 - 2 * flip, 0, n - 1) ^ q
    partner = jnp.clip(q - 1 + 2 * flip, 0, n - 1) ^ q
    order = jnp.stack([q, flip, partner])
    base = dict(rows=rows, tiles=tiles, eps=eps, n=n, space=space, index=None, d=0, vmem=12)
    if n != 4:
        xs = [slab(field, q)] + [swap(slab(field, q ^ d), d) for d in range(1, n)]
        x = jnp.concatenate(xs, axis=1)
        cfg = dict(base, whole=n * count, count=n * count, n_blocks=1, old=[], vmem=40)
        x = jnp.concatenate([x[:, :, t * LANES : (t + 1) * LANES] for t in range(tiles)], axis=0)
        _, total = phase(cfg, order, velocity, w, [x], [], None, None)
        send, here, send_row, own = lines_of([x], rows, tiles, order, (0, 0, 1))
        there = beside(send).reshape(rows // 2, n, count, LANES)
        there = there[:, jnp.arange(n) ^ source].reshape(send.shape)
        total = border(
            eps, [[0]], [[0]], order, velocity, weights, total,
            [here], [own], [above(send_row)], [there], space, n,
        )
        tiles = spread_out(total, n, space, q, count)
    else:
        half = count // 2
        p1, p3 = first_pack((1, 3), tiles, order, field)
        x1, x3 = swap(p1, 1), swap(p3, 3)
        jobs = [(0, "full", 0, 0), (2, "rim", 0, half), (2, "inner", half, count)]
        x0, p2, p2b = pack(jobs, tiles, order, after(field, p3))
        front, back = swap(p2, 2), swap(p2b, 2)
        base = dict(base, whole=count, n_blocks=n)
        names, old, g = [], [], None

        halo, halo1 = halos_of(n, tiles, order, after(field, p2b))
        there, met = [halo, swap(halo1, 1)], []

        def meet(arrays, choice):
            send, here, row, own = lines_of(arrays, rows, tiles, order, choice)
            met.append((here, own, above(row)))
            there.append(beside(send))

        x0 = after(x0, weights)
        for d, x in ((0, x0), (1, x1), (3, x3)):
            if names:
                x = after(x, g)
            if d == 3:
                meet([x0, x1, x], (2, 1, 3))
            cfg = dict(base, count=count, d=d, old=list(names))
            kept, g = phase(cfg, order, velocity, w, [x], old, None, g)
            names, old = [*names, d], [*old, (x, kept)]
        front = after(front, (g, met[-1][2]))
        meet([front, x0], (0, 1, 1))
        part = dict(base, d=2, count=half, old=names, index=0)
        kept = phase(part, order, velocity, w, [front], [], None, None)
        back = after(back, (kept[1], met[-1][2]))
        part = dict(part, index=1)
        (g,) = phase(part, order, velocity, w, [front, back], old, kept, g)
        met = [list(v) for v in zip(*met)]
        g = border(
            eps, [[0, 1, 3], [2]], [[0], [1], [2], [3]], order, velocity, weights, g,
            *met, there, space, n,
        )
        tiles = g
    arrived = lax.all_to_all(tiles, ("space", "mode"), split_axis=0, concat_axis=0, tiled=True)
    return jnp.sum(arrived.astype(F32), axis=0) * eps


def solution(mesh):
    placed = (P("mode", "space", None), P("space", None), P())
    return jax.shard_map(
        local, mesh=mesh, in_specs=placed, out_specs=P("space", "mode"), check_vma=False
    )
```

```python
import functools
import math

import jax
import jax.numpy as jnp
from jax import lax
from jax.experimental import pallas as pl
from jax.experimental.pallas import tpu as pltpu
from jax.sharding import PartitionSpec as P

NZ = 64
LANES = 128
SUB = 16
PACK_VMEM = 16
BF = jnp.bfloat16
F32 = jnp.float32
VMEM = pltpu.VMEM


def product(left, right):
    return lax.dot_general(left, right, (((1,), (1,)), ((), ())), preferred_element_type=F32)


def apply_rows(i, eps, velocity, w, xs, a, tiles, rows, off, count):
    span = rows + 2
    xp, xm = eps - 0.5 * velocity[0], eps + 0.5 * velocity[0]
    yp, ym = eps - 0.5 * velocity[1], eps + 0.5 * velocity[1]
    zp, zm = eps - 0.5 * velocity[2], eps + 0.5 * velocity[2]
    lane = lax.broadcasted_iota(jnp.int32, (SUB, LANES), 1)
    low = lane < NZ
    zps = jnp.where(lane % NZ == NZ - 1, 0.0, zp)
    zms = jnp.where(lane % NZ == 0, 0.0, zm)
    own = jnp.where(low, yp, ym)
    other = jnp.where(low, ym, yp)

    def body(j, carry):
        source = pl.ds(pl.multiple_of(j * SUB, SUB), SUB)
        target = pl.ds(pl.multiple_of(j * SUB + off, SUB), SUB)
        center = [
            [xs[t * span + 2 * i + r, source, :].astype(F32) for t in range(tiles)] for r in range(4)
        ]
        for r in (0, 1):
            mid = center[r + 1]
            turned = [pltpu.roll(c, NZ, 1) for c in mid]
            for t in range(tiles):
                c = mid[t]
                behind = turned[t + 1] if t + 1 < tiles else jnp.zeros_like(c)
                before = turned[t - 1] if t > 0 else jnp.zeros_like(c)
                value = xp * center[r + 2][t] + xm * center[r][t]
                value = value + own * turned[t] + other * jnp.where(low, before, behind)
                value = value + zps * pltpu.roll(c, LANES - 1, 1) + zms * pltpu.roll(c, 1, 1)
                value = (value - (6.0 * eps) * c) * w[2 * i + r, :, t * LANES : (t + 1) * LANES]
                a[t * rows + 2 * i + r, target, :] = value.astype(BF)
        return carry

    lax.fori_loop(0, count // SUB, body, 0)


def phase_kernel(cfg, *refs):
    refs = list(refs)
    take = lambda k: [refs.pop(0) for _ in range(k)]
    d, count, whole, index = cfg["d"], cfg["count"], cfg["whole"], cfg["index"]
    rows, tiles = cfg["rows"], cfg["tiles"]
    steps, span = rows // 2, rows + 2
    order, velocity, w = take(3)
    parts = take(cfg["n_parts"])
    old = [take(2) for _ in range(cfg["n_old"])]
    prev = take(2) if index == 1 else None
    gin = take(1)[0] if cfg["gin"] else None
    xo = take(1)[0] if index == 0 else None
    a = take(1)[0] if index != 1 else None
    gout = take(1)[0] if index != 0 else None
    if index == 1:
        (a,) = take(1)
    xs = take(1)[0]
    t2 = take(1)[0] if index != 0 else None
    t1 = take(1)[0] if old and index != 0 else None

    if index is not None:
        rim, inner = parts[0], parts[-1]
        deep = rows - 2
        begin = inner.shape[0] - (tiles - 2) * deep
        base = index * (2 * tiles + 2 * deep)
        sides = (base + 2 * tiles, base + 2 * tiles + deep)
    for t in range(tiles):
        xs[t * span] = jnp.zeros_like(xs[0])
        xs[t * span + rows + 1] = jnp.zeros_like(xs[0])
        if index is not None:
            xs[t * span + 1] = rim[base + t]
            xs[t * span + rows] = rim[base + tiles + t]
            if t in (0, tiles - 1):
                first = sides[t // (tiles - 1)]
                xs[t * span + 2 : t * span + rows] = rim[first : first + deep]
            else:
                xs[t * span + 2 : t * span + rows] = inner[begin + (t - 1) * deep : begin + t * deep]
        else:
            xs[t * span + 1 : t * span + rows + 1] = parts[0][t * rows : (t + 1) * rows]

    def stencil(i, carry):
        apply_rows(i, cfg["eps"], velocity, w, xs, a, tiles, rows, 0, count)
        return carry

    lax.fori_loop(0, steps, stencil, 0)
    if index == 0:
        for t in range(tiles):
            xo[t * rows : (t + 1) * rows] = xs[t * span + 1 : t * span + rows + 1]
        return

    t2[...] = jnp.zeros_like(t2)
    if t1 is not None:
        t1[...] = jnp.zeros_like(t1)

    def body(i, carry):
        pairs = [(r, t) for r in (0, 1) for t in range(tiles)]
        picks = [t * rows + 2 * i + r for r, t in pairs]
        join = lambda pieces: jnp.concatenate(pieces, axis=1)
        wide = lambda ref: join([ref[k] for k in picks])
        new = join([xs[t * span + 2 * i + r + 1] for r, t in pairs])
        mark = wide(a)
        if prev is not None:
            new = jnp.concatenate([wide(prev[0]), new], axis=0)
            mark = jnp.concatenate([wide(prev[1]), mark], axis=0)
        t2[...] += product(jnp.concatenate([wide(ox) for ox, _ in old] + [new], axis=0), mark)
        if old:
            t1[...] += product(jnp.concatenate([wide(oa) for _, oa in old], axis=0), new)
        return carry

    lax.fori_loop(0, steps, body, 0)

    gout[...] = jnp.zeros_like(gout) if gin is None else gin[...]
    block = lambda k: slice(k * whole, (k + 1) * whole)
    for k, o in enumerate([*cfg["old"], d]):
        gout[block(o), block(d)] += t2[block(k), :]
        if o != d:
            gout[block(d), block(o)] += t1[block(k), :].T


def phase(cfg, order, velocity, w, parts, old, prev, gin):
    rows, tiles, whole, count = cfg["rows"], cfg["tiles"], cfg["whole"], cfg["count"]
    size, index = cfg["n_blocks"] * whole, cfg["index"]
    kept = jax.ShapeDtypeStruct((tiles * rows, count, LANES), BF)
    total = jax.ShapeDtypeStruct((size, size), F32)
    args = [order, velocity, w, *parts]
    for group in [*old, *([prev] if prev is not None else [])]:
        args += list(group)
    if gin is not None:
        args.append(gin)
    out_shape = {None: [kept, total], 0: [kept, kept], 1: [total]}[index]
    scratch = [VMEM(kept.shape, BF)] if index == 1 else []
    scratch.append(VMEM((tiles * (rows + 2), count, LANES), BF))
    if index != 0:
        scratch.append(VMEM(((len(old) + 1) * whole, whole), F32))
        if old:
            scratch.append(VMEM((len(old) * whole, whole), F32))
    cfg = dict(cfg, n_parts=len(parts), n_old=len(old), gin=gin is not None)
    vmem = pl.BlockSpec(memory_space=VMEM)
    smem = pl.BlockSpec(memory_space=pltpu.SMEM)
    return pl.pallas_call(
        functools.partial(phase_kernel, cfg),
        in_specs=[smem, smem] + [vmem] * (len(args) - 2),
        out_specs=[vmem] * len(out_shape),
        out_shape=out_shape,
        scratch_shapes=scratch,
        compiler_params=pltpu.CompilerParams(vmem_limit_bytes=cfg["vmem"] << 20),
        cost_estimate=pl.CostEstimate(flops=1, bytes_accessed=1, transcendentals=0),
    )(*args)


def line_kernel(rows, tiles, choice, order, *refs):
    ins, (near, far, near_row, far_row) = refs[:-4], refs[-4:]
    deep = rows - 2
    keep = order[1] == 0

    def tile_row(ref, row, t, c):
        if c is None:
            return ref[t * rows + row].astype(F32)
        base = c * (2 * tiles + 2 * deep)
        if row in (0, rows - 1):
            return ref[base + (tiles if row else 0) + t].astype(F32)
        return ref[base + 2 * tiles + (deep if t else 0) + row - 1].astype(F32)

    def parts_of(ref):
        return [(ref, None)] if ref.shape[0] == tiles * rows else [(ref, 0), (ref, 1)]

    def line(ref, c, i, first):
        t = 0 if first else tiles - 1
        low = lax.broadcasted_iota(jnp.int32, (ref.shape[1], LANES), 1) < NZ
        one, two = tile_row(ref, 2 * i, t, c), tile_row(ref, 2 * i + 1, t, c)
        if first:
            return jnp.where(low, one, pltpu.roll(two, NZ, 1))
        return jnp.where(low, pltpu.roll(one, NZ, 1), two)

    start = 0
    for ref in ins[: choice[2]]:
        for ref, c in parts_of(ref):
            modes = slice(start, start + ref.shape[1])
            start += ref.shape[1]
            for t in range(tiles):
                near_row[t, modes, :] = tile_row(ref, 0, t, c).astype(BF)
                far_row[t, modes, :] = tile_row(ref, rows - 1, t, c).astype(BF)
            for i in range(rows // 2):
                value = jnp.where(keep, line(ref, c, i, False), line(ref, c, i, True))
                far[i, modes, :] = value.astype(BF)

    def send(ref):
        start = 0
        for ref, c in parts_of(ref):
            modes = slice(start, start + ref.shape[1])
            start += ref.shape[1]
            for i in range(rows // 2):
                value = jnp.where(keep, line(ref, c, i, True), line(ref, c, i, False))
                near[i, modes, :] = value.astype(BF)

    if choice[0] == choice[1]:
        send(ins[choice[0]])
    else:
        pl.when(order[2] == 1)(lambda: send(ins[choice[0]]))
        pl.when(order[2] != 1)(lambda: send(ins[choice[1]]))


def lines_of(arrays, rows, tiles, order, choice):
    size = lambda v: v.shape[1] * (1 if v.shape[0] == tiles * rows else 2)
    modes = sum(size(v) for v in arrays[: choice[2]])
    vmem = pl.BlockSpec(memory_space=VMEM)
    lines = lambda m: jax.ShapeDtypeStruct((rows // 2, m, LANES), BF)
    row = jax.ShapeDtypeStruct((tiles, modes, LANES), BF)
    return pl.pallas_call(
        functools.partial(line_kernel, rows, tiles, choice),
        in_specs=[pl.BlockSpec(memory_space=pltpu.SMEM)] + [vmem] * len(arrays),
        out_specs=[vmem] * 4,
        out_shape=[lines(size(arrays[choice[0]])), lines(modes), row, row],
        compiler_params=pltpu.CompilerParams(vmem_limit_bytes=12 << 20),
        cost_estimate=pl.CostEstimate(flops=1, bytes_accessed=1, transcendentals=0),
    )(order, *arrays)


def halo_kernel(n, tiles, order, field, *refs):
    outs, (line, sem) = refs[:2], refs[2:]
    q, flip = order[0], order[1]
    copies = []
    for d in (0, 1):
        owner = q ^ d
        at = jnp.where(
            flip == 0,
            jnp.minimum((owner + 1) * tiles, n * tiles - 1),
            jnp.maximum(owner * tiles - 1, 0),
        )
        at = pl.ds(pl.multiple_of(at * LANES, LANES), LANES)
        copies.append(pltpu.make_async_copy(field.at[:, :, at], line.at[d], sem.at[d]))
        copies[-1].start()
    low = lax.broadcasted_iota(jnp.int32, line.shape[2:], 1) < NZ
    for d in (0, 1):
        copies[d].wait()
        owner = q ^ d
        none = jnp.where(flip == 0, owner == n - 1, owner == 0)
        for i in range(line.shape[1] // 2):
            one, two = line[d, 2 * i].astype(F32), line[d, 2 * i + 1].astype(F32)
            front = jnp.where(low, one, pltpu.roll(two, NZ, 1))
            back = jnp.where(low, pltpu.roll(one, NZ, 1), two)
            value = jnp.where(flip == 0, front, back)
            outs[d][i] = jnp.where(none, 0.0, value).astype(BF)


def halos_of(n, tiles, order, field):
    rows, count, _ = field.shape
    shape = jax.ShapeDtypeStruct((rows // 2, count, LANES), BF)
    return pl.pallas_call(
        functools.partial(halo_kernel, n, tiles),
        in_specs=[pl.BlockSpec(memory_space=pltpu.SMEM), pl.BlockSpec(memory_space=pl.ANY)],
        out_specs=[pl.BlockSpec(memory_space=VMEM)] * 2,
        out_shape=[shape] * 2,
        scratch_shapes=[VMEM((2, rows, count, LANES), BF), pltpu.SemaphoreType.DMA((2,))],
        compiler_params=pltpu.CompilerParams(vmem_limit_bytes=12 << 20),
        cost_estimate=pl.CostEstimate(flops=1, bytes_accessed=1, transcendentals=0),
    )(order, field)


def border_kernel(eps, groups, beyond, space, n, order, velocity, wn, wh, wr, wx, gin, *refs):
    count = len(groups)
    here, own, over = refs[:count], refs[count : 2 * count], refs[2 * count : 3 * count]
    there, (out, g) = refs[3 * count : -2], refs[-2:]
    xp, xm = eps - 0.5 * velocity[0], eps + 0.5 * velocity[0]
    yp, ym = eps - 0.5 * velocity[1], eps + 0.5 * velocity[1]
    toward = jnp.where(order[1] == 0, yp, ym)
    back = jnp.where(order[1] == 0, ym, yp)
    blocks = sum(len(names) for names in groups)
    size = g.shape[0] // blocks

    def find(refs, d, i, groups=groups):
        for names, ref in zip(groups, refs):
            if d in names:
                k = names.index(d)
                return ref[i, k * size : (k + 1) * size, :]

    def every(refs, i, groups=groups):
        return jnp.concatenate([find(refs, d, i, groups) for d in range(blocks)], axis=0)

    left, right = [], []
    for k in range(wn.shape[0]):
        mine = every(here, k)
        other = every(there, k, beyond).astype(F32)
        left += [mine, other.astype(BF)]
        right += [(wn[k] * (toward * other)).astype(BF), (wh[k] * (back * mine.astype(F32))).astype(BF)]
    for t in range(wr.shape[0]):
        mine, other = every(own, t), every(over, t)
        left += [mine, other]
        right += [
            (wr[t] * (xp * other.astype(F32))).astype(BF),
            (wx[t] * (xm * mine.astype(F32))).astype(BF),
        ]
    total = gin[...]
    for k in range(0, len(left), 4):
        total = total + product(
            jnp.concatenate(left[k : k + 4], axis=1), jnp.concatenate(right[k : k + 4], axis=1)
        )
    g[...] = total
    if blocks == n:
        q = order[0]
        share = out.shape[1]
        per = size // share
        for s in range(space):
            first = pl.multiple_of(((s // per) ^ q) * size + (s % per) * share, share)
            for z in range(n):
                start = pl.multiple_of((z ^ q) * size, size)
                out[s * n + z] = g[pl.ds(first, share), pl.ds(start, size)].astype(out.dtype)
    else:
        out[...] = total


def border(eps, groups, beyond, order, velocity, weights, gin, here, own, over, there, space, n):
    vmem = pl.BlockSpec(memory_space=VMEM)
    smem = pl.BlockSpec(memory_space=pltpu.SMEM)
    blocks = sum(len(names) for names in groups)
    shape = jax.ShapeDtypeStruct(gin.shape, F32)
    if blocks == n:
        size = gin.shape[0]
        shape = jax.ShapeDtypeStruct((space * n, size // space, size // n), BF)
    args = [order, velocity, *weights, gin, *here, *own, *over, *there]
    return pl.pallas_call(
        functools.partial(border_kernel, eps, groups, beyond, space, n),
        in_specs=[smem, smem] + [vmem] * (len(args) - 2),
        out_specs=vmem,
        out_shape=shape,
        scratch_shapes=[VMEM(gin.shape, F32)],
        compiler_params=pltpu.CompilerParams(vmem_limit_bytes=16 << 20),
        cost_estimate=pl.CostEstimate(flops=1, bytes_accessed=1, transcendentals=0),
    )(*args)


def pack_kernel(jobs, rows, tiles, order, field, *refs):
    outs, sem = refs[:-1], refs[-1]
    q = order[0]
    deep = rows - 2
    copies = []
    for k, (d, kind, a, b) in enumerate(jobs):
        base = (q ^ d) * tiles * LANES
        cut = lambda t: pl.ds(pl.multiple_of(base + t * LANES, LANES), LANES)
        for t in range(tiles):
            if kind == "full":
                copies.append((field.at[:, :, cut(t)], outs[k].at[t * rows : (t + 1) * rows]))
                continue
            inside = slice(1, rows - 1)
            if t not in (0, tiles - 1):
                begin = 2 * (2 * tiles + 2 * deep) if kind == "rim" else 0
                to = slice(begin + (t - 1) * deep, begin + t * deep)
                copies.append((field.at[inside, a:b, cut(t)], outs[k].at[to]))
            if kind == "rim":
                for c in (0, 1):
                    first = c * (2 * tiles + 2 * deep)
                    half = slice(c * (b - a), (c + 1) * (b - a))
                    copies.append((field.at[0, half, cut(t)], outs[k].at[first + t]))
                    copies.append((field.at[rows - 1, half, cut(t)], outs[k].at[first + tiles + t]))
                    if t in (0, tiles - 1):
                        to = first + 2 * tiles + (deep if t else 0)
                        copies.append((field.at[inside, half, cut(t)], outs[k].at[to : to + deep]))
    copies = [pltpu.make_async_copy(src, dst, sem.at[m]) for m, (src, dst) in enumerate(copies)]
    for c in copies:
        c.start()
    for c in copies:
        c.wait()


def pack(jobs, tiles, order, field):
    rows, count, _ = field.shape
    deep = rows - 2
    shapes, pieces = [], 0
    for d, kind, a, b in jobs:
        if kind == "full":
            shapes.append((tiles * rows, count, LANES))
            pieces += tiles
        else:
            length = (tiles - 2) * deep
            pieces += tiles - 2
            if kind == "rim":
                length += 2 * (2 * tiles + 2 * deep)
                pieces += 4 * tiles + 4
            shapes.append((length, b - a, LANES))
    anywhere = pl.BlockSpec(memory_space=pl.ANY)
    return pl.pallas_call(
        functools.partial(pack_kernel, jobs, rows, tiles),
        in_specs=[pl.BlockSpec(memory_space=pltpu.SMEM), anywhere],
        out_specs=[anywhere] * len(jobs),
        out_shape=[jax.ShapeDtypeStruct(s, BF) for s in shapes],
        scratch_shapes=[pltpu.SemaphoreType.DMA((pieces,))],
        compiler_params=pltpu.CompilerParams(vmem_limit_bytes=PACK_VMEM << 20),
    )(order, field)


def first_kernel(owners, rows, tiles, order, field, *refs):
    count = len(owners)
    outs, (stage, into, out_of) = refs[:count], refs[count:]
    loads, stores = [], []
    for k, d in enumerate(owners):
        wide = pl.ds(pl.multiple_of((order[0] ^ d) * tiles * LANES, LANES), tiles * LANES)
        loads.append(pltpu.make_async_copy(field.at[:, :, wide], stage.at[k], into.at[k]))
        loads[-1].start()
    for k in range(count):
        loads[k].wait()
        for t in range(tiles):
            lanes = slice(t * LANES, (t + 1) * LANES)
            to = outs[k].at[t * rows : (t + 1) * rows]
            stores.append(
                pltpu.make_async_copy(stage.at[k, :, :, lanes], to, out_of.at[k * tiles + t])
            )
            stores[-1].start()
    for c in stores:
        c.wait()


def first_pack(owners, tiles, order, field):
    rows, count, _ = field.shape
    shape = jax.ShapeDtypeStruct((tiles * rows, count, LANES), BF)
    anywhere = pl.BlockSpec(memory_space=pl.ANY)
    return pl.pallas_call(
        functools.partial(first_kernel, owners, rows, tiles),
        in_specs=[pl.BlockSpec(memory_space=pltpu.SMEM), anywhere],
        out_specs=[anywhere] * len(owners),
        out_shape=[shape] * len(owners),
        scratch_shapes=[
            VMEM((len(owners), rows, count, tiles * LANES), BF),
            pltpu.SemaphoreType.DMA((len(owners),)),
            pltpu.SemaphoreType.DMA((len(owners) * tiles,)),
        ],
        compiler_params=pltpu.CompilerParams(vmem_limit_bytes=60 << 20),
    )(order, field)


def spread_out(total, n, space, q, count):
    share = n * count // space
    out = []
    for s in range(space):
        start = ((s * share) // count ^ q) * count + (s * share) % count
        rows = lax.dynamic_slice_in_dim(total, start, share, axis=0)
        out += [lax.dynamic_slice_in_dim(rows, (z ^ q) * count, count, axis=1) for z in range(n)]
    return jnp.stack(out)


def after(value, token):
    return lax.optimization_barrier((value, token))[0]


def local(modes, phases, velocity):
    space, n = lax.axis_size("space"), lax.axis_size("mode")
    sp, q = lax.axis_index("space"), lax.axis_index("mode")
    count, rows, plane = modes.shape
    width = plane // n
    tiles = width // LANES
    eps = 1.0 / math.sqrt(space * rows * plane)
    field = jnp.transpose(modes, (1, 0, 2))
    flip = sp & 1

    weight = jnp.where(phases == 0, 0.1, jnp.where(phases == 1, 1.0, 0.5)).astype(F32)
    w = lax.dynamic_slice_in_dim(weight, q * width, width, axis=1)[:, None, :]

    near = jnp.where(flip == 0, jnp.minimum((q + 1) * width, plane - NZ), jnp.maximum(q * width - NZ, 0))
    mine = jnp.where(flip == 0, (q + 1) * width - NZ, q * width)
    wh, wn = [
        lax.dynamic_slice_in_dim(weight, v, NZ, axis=1).reshape(rows // 2, 1, LANES)
        for v in (near, mine)
    ]

    def slab(source, owner):
        return lax.dynamic_slice_in_dim(source, owner * width, width, axis=2)

    ahead = [(i + 1, i) for i in range(space - 1)]
    above = lambda v: lax.ppermute(v, "space", ahead)
    cut = lambda v: lax.dynamic_slice_in_dim(v, q * width, width, axis=1).reshape(tiles, 1, LANES)
    weights = (wn, wh, cut(weight[rows - 1 :]), cut(above(weight[:1])))

    def swap(part, d):
        return lax.ppermute(part, "mode", [(i, i ^ d) for i in range(n)])

    relay = [(s * n + i, s * n + i - 1 + 2 * (s & 1)) for s in range(space) for i in range(n)]
    relay = [(i, j) for i, j in relay if i // n == j // n and j >= 0]
    beside = lambda v: lax.ppermute(v, ("space", "mode"), relay)
    source = jnp.clip(q + 1 - 2 * flip, 0, n - 1) ^ q
    partner = jnp.clip(q - 1 + 2 * flip, 0, n - 1) ^ q
    order = jnp.stack([q, flip, partner])
    base = dict(rows=rows, tiles=tiles, eps=eps, n=n, space=space, index=None, d=0, vmem=12)
    if n != 4:
        xs = [slab(field, q)] + [swap(slab(field, q ^ d), d) for d in range(1, n)]
        x = jnp.concatenate(xs, axis=1)
        cfg = dict(base, whole=n * count, count=n * count, n_blocks=1, old=[], vmem=40)
        x = jnp.concatenate([x[:, :, t * LANES : (t + 1) * LANES] for t in range(tiles)], axis=0)
        _, total = phase(cfg, order, velocity, w, [x], [], None, None)
        send, here, send_row, own = lines_of([x], rows, tiles, order, (0, 0, 1))
        there = beside(send).reshape(rows // 2, n, count, LANES)
        there = there[:, jnp.arange(n) ^ source].reshape(send.shape)
        total = border(
            eps, [[0]], [[0]], order, velocity, weights, total,
            [here], [own], [above(send_row)], [there], space, n,
        )
        tiles = spread_out(total, n, space, q, count)
    else:
        half = count // 2
        p1, p3 = first_pack((1, 3), tiles, order, field)
        x1, x3 = swap(p1, 1), swap(p3, 3)
        jobs = [(0, "full", 0, 0), (2, "rim", 0, half), (2, "inner", half, count)]
        x0, p2, p2b = pack(jobs, tiles, order, after(field, p3))
        front, back = swap(p2, 2), swap(p2b, 2)
        base = dict(base, whole=count, n_blocks=n)
        names, old, g = [], [], None

        halo, halo1 = halos_of(n, tiles, order, after(field, p2b))
        there, met = [halo, swap(halo1, 1)], []

        def meet(arrays, choice):
            send, here, row, own = lines_of(arrays, rows, tiles, order, choice)
            met.append((here, own, above(row)))
            there.append(beside(send))

        x0 = after(x0, weights)
        for d, x in ((0, x0), (3, x3), (1, x1)):
            if names:
                x = after(x, g)
            if d == 1:
                meet([x0, x3, x], (1, 2, 3))
            cfg = dict(base, count=count, d=d, old=list(names))
            kept, g = phase(cfg, order, velocity, w, [x], old, None, g)
            names, old = [*names, d], [*old, (x, kept)]
        front = after(front, (g, met[-1][2]))
        meet([front, x0], (0, 1, 1))
        part = dict(base, d=2, count=half, old=names, index=0)
        kept = phase(part, order, velocity, w, [front], [], None, None)
        back = after(back, (kept[1], met[-1][2]))
        part = dict(part, index=1)
        (g,) = phase(part, order, velocity, w, [front, back], old, kept, g)
        met = [list(v) for v in zip(*met)]
        g = border(
            eps, [[0, 3, 1], [2]], [[0], [1], [2], [3]], order, velocity, weights, g,
            *met, there, space, n,
        )
        tiles = g
    arrived = lax.all_to_all(tiles, ("space", "mode"), split_axis=0, concat_axis=0, tiled=True)
    return jnp.sum(arrived.astype(F32), axis=0) * eps


def solution(mesh):
    placed = (P("mode", "space", None), P("space", None), P())
    return jax.shard_map(
        local, mesh=mesh, in_specs=placed, out_specs=P("space", "mode"), check_vma=False
    )
```

```python
import functools
import math

import jax
import jax.numpy as jnp
from jax import lax
from jax.experimental import pallas as pl
from jax.experimental.pallas import tpu as pltpu
from jax.sharding import PartitionSpec as P

NZ = 64
LANES = 128
SUB = 16
PACK_VMEM = 16
BF = jnp.bfloat16
F32 = jnp.float32
VMEM = pltpu.VMEM


def product(left, right):
    return lax.dot_general(left, right, (((1,), (1,)), ((), ())), preferred_element_type=F32)


def apply_rows(i, eps, velocity, w, xs, a, tiles, rows, off, count):
    span = rows + 2
    xp, xm = eps - 0.5 * velocity[0], eps + 0.5 * velocity[0]
    yp, ym = eps - 0.5 * velocity[1], eps + 0.5 * velocity[1]
    zp, zm = eps - 0.5 * velocity[2], eps + 0.5 * velocity[2]
    lane = lax.broadcasted_iota(jnp.int32, (SUB, LANES), 1)
    low = lane < NZ
    zps = jnp.where(lane % NZ == NZ - 1, 0.0, zp)
    zms = jnp.where(lane % NZ == 0, 0.0, zm)
    own = jnp.where(low, yp, ym)
    other = jnp.where(low, ym, yp)

    def body(j, carry):
        source = pl.ds(pl.multiple_of(j * SUB, SUB), SUB)
        target = pl.ds(pl.multiple_of(j * SUB + off, SUB), SUB)
        center = [
            [xs[t * span + 2 * i + r, source, :].astype(F32) for t in range(tiles)] for r in range(4)
        ]
        for r in (0, 1):
            mid = center[r + 1]
            turned = [pltpu.roll(c, NZ, 1) for c in mid]
            for t in range(tiles):
                c = mid[t]
                behind = turned[t + 1] if t + 1 < tiles else jnp.zeros_like(c)
                before = turned[t - 1] if t > 0 else jnp.zeros_like(c)
                value = xp * center[r + 2][t] + xm * center[r][t]
                value = value + own * turned[t] + other * jnp.where(low, before, behind)
                value = value + zps * pltpu.roll(c, LANES - 1, 1) + zms * pltpu.roll(c, 1, 1)
                value = (value - (6.0 * eps) * c) * w[2 * i + r, :, t * LANES : (t + 1) * LANES]
                a[t * rows + 2 * i + r, target, :] = value.astype(BF)
        return carry

    lax.fori_loop(0, count // SUB, body, 0, unroll=4)


def phase_kernel(cfg, *refs):
    refs = list(refs)
    take = lambda k: [refs.pop(0) for _ in range(k)]
    d, count, whole, index = cfg["d"], cfg["count"], cfg["whole"], cfg["index"]
    rows, tiles = cfg["rows"], cfg["tiles"]
    steps, span = rows // 2, rows + 2
    order, velocity, w = take(3)
    parts = take(cfg["n_parts"])
    old = [take(2) for _ in range(cfg["n_old"])]
    prev = take(2) if index == 1 else None
    gin = take(1)[0] if cfg["gin"] else None
    xo = take(1)[0] if index == 0 else None
    a = take(1)[0] if index != 1 else None
    gout = take(1)[0] if index != 0 else None
    if index == 1:
        (a,) = take(1)
    xs = take(1)[0]
    t2 = take(1)[0] if index != 0 else None
    t1 = take(1)[0] if old and index != 0 else None

    if index is not None:
        rim, inner = parts[0], parts[-1]
        deep = rows - 2
        begin = inner.shape[0] - (tiles - 2) * deep
        base = index * (2 * tiles + 2 * deep)
        sides = (base + 2 * tiles, base + 2 * tiles + deep)
    for t in range(tiles):
        xs[t * span] = jnp.zeros_like(xs[0])
        xs[t * span + rows + 1] = jnp.zeros_like(xs[0])
        if index is not None:
            xs[t * span + 1] = rim[base + t]
            xs[t * span + rows] = rim[base + tiles + t]
            if t in (0, tiles - 1):
                first = sides[t // (tiles - 1)]
                xs[t * span + 2 : t * span + rows] = rim[first : first + deep]
            else:
                xs[t * span + 2 : t * span + rows] = inner[begin + (t - 1) * deep : begin + t * deep]
        else:
            xs[t * span + 1 : t * span + rows + 1] = parts[0][t * rows : (t + 1) * rows]

    def stencil(i, carry):
        apply_rows(i, cfg["eps"], velocity, w, xs, a, tiles, rows, 0, count)
        return carry

    lax.fori_loop(0, steps, stencil, 0)
    if index == 0:
        for t in range(tiles):
            xo[t * rows : (t + 1) * rows] = xs[t * span + 1 : t * span + rows + 1]
        return

    t2[...] = jnp.zeros_like(t2)
    if t1 is not None:
        t1[...] = jnp.zeros_like(t1)

    def body(i, carry):
        pairs = [(r, t) for r in (0, 1) for t in range(tiles)]
        picks = [t * rows + 2 * i + r for r, t in pairs]
        join = lambda pieces: jnp.concatenate(pieces, axis=1)
        wide = lambda ref: join([ref[k] for k in picks])
        new = join([xs[t * span + 2 * i + r + 1] for r, t in pairs])
        mark = wide(a)
        if prev is not None:
            new = jnp.concatenate([wide(prev[0]), new], axis=0)
            mark = jnp.concatenate([wide(prev[1]), mark], axis=0)
        t2[...] += product(jnp.concatenate([wide(ox) for ox, _ in old] + [new], axis=0), mark)
        if old:
            t1[...] += product(jnp.concatenate([wide(oa) for _, oa in old], axis=0), new)
        return carry

    lax.fori_loop(0, steps, body, 0)

    gout[...] = jnp.zeros_like(gout) if gin is None else gin[...]
    block = lambda k: slice(k * whole, (k + 1) * whole)
    for k, o in enumerate([*cfg["old"], d]):
        gout[block(o), block(d)] += t2[block(k), :]
        if o != d:
            gout[block(d), block(o)] += t1[block(k), :].T


def phase(cfg, order, velocity, w, parts, old, prev, gin):
    rows, tiles, whole, count = cfg["rows"], cfg["tiles"], cfg["whole"], cfg["count"]
    size, index = cfg["n_blocks"] * whole, cfg["index"]
    kept = jax.ShapeDtypeStruct((tiles * rows, count, LANES), BF)
    total = jax.ShapeDtypeStruct((size, size), F32)
    args = [order, velocity, w, *parts]
    for group in [*old, *([prev] if prev is not None else [])]:
        args += list(group)
    if gin is not None:
        args.append(gin)
    out_shape = {None: [kept, total], 0: [kept, kept], 1: [total]}[index]
    scratch = [VMEM(kept.shape, BF)] if index == 1 else []
    scratch.append(VMEM((tiles * (rows + 2), count, LANES), BF))
    if index != 0:
        scratch.append(VMEM(((len(old) + 1) * whole, whole), F32))
        if old:
            scratch.append(VMEM((len(old) * whole, whole), F32))
    cfg = dict(cfg, n_parts=len(parts), n_old=len(old), gin=gin is not None)
    vmem = pl.BlockSpec(memory_space=VMEM)
    smem = pl.BlockSpec(memory_space=pltpu.SMEM)
    return pl.pallas_call(
        functools.partial(phase_kernel, cfg),
        in_specs=[smem, smem] + [vmem] * (len(args) - 2),
        out_specs=[vmem] * len(out_shape),
        out_shape=out_shape,
        scratch_shapes=scratch,
        compiler_params=pltpu.CompilerParams(vmem_limit_bytes=cfg["vmem"] << 20),
        cost_estimate=pl.CostEstimate(flops=1, bytes_accessed=1, transcendentals=0),
    )(*args)


def line_kernel(rows, tiles, choice, order, *refs):
    ins, (near, far, near_row, far_row) = refs[:-4], refs[-4:]
    deep = rows - 2
    keep = order[1] == 0

    def tile_row(ref, row, t, c):
        if c is None:
            return ref[t * rows + row].astype(F32)
        base = c * (2 * tiles + 2 * deep)
        if row in (0, rows - 1):
            return ref[base + (tiles if row else 0) + t].astype(F32)
        return ref[base + 2 * tiles + (deep if t else 0) + row - 1].astype(F32)

    def parts_of(ref):
        return [(ref, None)] if ref.shape[0] == tiles * rows else [(ref, 0), (ref, 1)]

    def line(ref, c, i, first):
        t = 0 if first else tiles - 1
        low = lax.broadcasted_iota(jnp.int32, (ref.shape[1], LANES), 1) < NZ
        one, two = tile_row(ref, 2 * i, t, c), tile_row(ref, 2 * i + 1, t, c)
        if first:
            return jnp.where(low, one, pltpu.roll(two, NZ, 1))
        return jnp.where(low, pltpu.roll(one, NZ, 1), two)

    start = 0
    for ref in ins[: choice[2]]:
        for ref, c in parts_of(ref):
            modes = slice(start, start + ref.shape[1])
            start += ref.shape[1]
            for t in range(tiles):
                near_row[t, modes, :] = tile_row(ref, 0, t, c).astype(BF)
                far_row[t, modes, :] = tile_row(ref, rows - 1, t, c).astype(BF)
            for i in range(rows // 2):
                value = jnp.where(keep, line(ref, c, i, False), line(ref, c, i, True))
                far[i, modes, :] = value.astype(BF)

    def send(ref):
        start = 0
        for ref, c in parts_of(ref):
            modes = slice(start, start + ref.shape[1])
            start += ref.shape[1]
            for i in range(rows // 2):
                value = jnp.where(keep, line(ref, c, i, True), line(ref, c, i, False))
                near[i, modes, :] = value.astype(BF)

    if choice[0] == choice[1]:
        send(ins[choice[0]])
    else:
        pl.when(order[2] == 1)(lambda: send(ins[choice[0]]))
        pl.when(order[2] != 1)(lambda: send(ins[choice[1]]))


def lines_of(arrays, rows, tiles, order, choice):
    size = lambda v: v.shape[1] * (1 if v.shape[0] == tiles * rows else 2)
    modes = sum(size(v) for v in arrays[: choice[2]])
    vmem = pl.BlockSpec(memory_space=VMEM)
    lines = lambda m: jax.ShapeDtypeStruct((rows // 2, m, LANES), BF)
    row = jax.ShapeDtypeStruct((tiles, modes, LANES), BF)
    return pl.pallas_call(
        functools.partial(line_kernel, rows, tiles, choice),
        in_specs=[pl.BlockSpec(memory_space=pltpu.SMEM)] + [vmem] * len(arrays),
        out_specs=[vmem] * 4,
        out_shape=[lines(size(arrays[choice[0]])), lines(modes), row, row],
        compiler_params=pltpu.CompilerParams(vmem_limit_bytes=12 << 20),
        cost_estimate=pl.CostEstimate(flops=1, bytes_accessed=1, transcendentals=0),
    )(order, *arrays)


def halo_kernel(n, tiles, order, field, *refs):
    outs, (line, sem) = refs[:2], refs[2:]
    q, flip = order[0], order[1]
    copies = []
    for d in (0, 1):
        owner = q ^ d
        at = jnp.where(
            flip == 0,
            jnp.minimum((owner + 1) * tiles, n * tiles - 1),
            jnp.maximum(owner * tiles - 1, 0),
        )
        at = pl.ds(pl.multiple_of(at * LANES, LANES), LANES)
        copies.append(pltpu.make_async_copy(field.at[:, :, at], line.at[d], sem.at[d]))
        copies[-1].start()
    low = lax.broadcasted_iota(jnp.int32, line.shape[2:], 1) < NZ
    for d in (0, 1):
        copies[d].wait()
        owner = q ^ d
        none = jnp.where(flip == 0, owner == n - 1, owner == 0)
        for i in range(line.shape[1] // 2):
            one, two = line[d, 2 * i].astype(F32), line[d, 2 * i + 1].astype(F32)
            front = jnp.where(low, one, pltpu.roll(two, NZ, 1))
            back = jnp.where(low, pltpu.roll(one, NZ, 1), two)
            value = jnp.where(flip == 0, front, back)
            outs[d][i] = jnp.where(none, 0.0, value).astype(BF)


def halos_of(n, tiles, order, field):
    rows, count, _ = field.shape
    shape = jax.ShapeDtypeStruct((rows // 2, count, LANES), BF)
    return pl.pallas_call(
        functools.partial(halo_kernel, n, tiles),
        in_specs=[pl.BlockSpec(memory_space=pltpu.SMEM), pl.BlockSpec(memory_space=pl.ANY)],
        out_specs=[pl.BlockSpec(memory_space=VMEM)] * 2,
        out_shape=[shape] * 2,
        scratch_shapes=[VMEM((2, rows, count, LANES), BF), pltpu.SemaphoreType.DMA((2,))],
        compiler_params=pltpu.CompilerParams(vmem_limit_bytes=12 << 20),
        cost_estimate=pl.CostEstimate(flops=1, bytes_accessed=1, transcendentals=0),
    )(order, field)


def border_kernel(eps, groups, beyond, space, n, order, velocity, wn, wh, wr, wx, gin, *refs):
    count = len(groups)
    here, own, over = refs[:count], refs[count : 2 * count], refs[2 * count : 3 * count]
    there, (out, g) = refs[3 * count : -2], refs[-2:]
    xp, xm = eps - 0.5 * velocity[0], eps + 0.5 * velocity[0]
    yp, ym = eps - 0.5 * velocity[1], eps + 0.5 * velocity[1]
    toward = jnp.where(order[1] == 0, yp, ym)
    back = jnp.where(order[1] == 0, ym, yp)
    blocks = sum(len(names) for names in groups)
    size = g.shape[0] // blocks

    def find(refs, d, i, groups=groups):
        for names, ref in zip(groups, refs):
            if d in names:
                k = names.index(d)
                return ref[i, k * size : (k + 1) * size, :]

    def every(refs, i, groups=groups):
        return jnp.concatenate([find(refs, d, i, groups) for d in range(blocks)], axis=0)

    left, right = [], []
    for k in range(wn.shape[0]):
        mine = every(here, k)
        other = every(there, k, beyond).astype(F32)
        left += [mine, other.astype(BF)]
        right += [(wn[k] * (toward * other)).astype(BF), (wh[k] * (back * mine.astype(F32))).astype(BF)]
    for t in range(wr.shape[0]):
        mine, other = every(own, t), every(over, t)
        left += [mine, other]
        right += [
            (wr[t] * (xp * other.astype(F32))).astype(BF),
            (wx[t] * (xm * mine.astype(F32))).astype(BF),
        ]
    total = gin[...]
    for k in range(0, len(left), 4):
        total = total + product(
            jnp.concatenate(left[k : k + 4], axis=1), jnp.concatenate(right[k : k + 4], axis=1)
        )
    g[...] = total
    if blocks == n:
        q = order[0]
        share = out.shape[1]
        per = size // share
        for s in range(space):
            first = pl.multiple_of(((s // per) ^ q) * size + (s % per) * share, share)
            for z in range(n):
                start = pl.multiple_of((z ^ q) * size, size)
                out[s * n + z] = g[pl.ds(first, share), pl.ds(start, size)].astype(out.dtype)
    else:
        out[...] = total


def border(eps, groups, beyond, order, velocity, weights, gin, here, own, over, there, space, n):
    vmem = pl.BlockSpec(memory_space=VMEM)
    smem = pl.BlockSpec(memory_space=pltpu.SMEM)
    blocks = sum(len(names) for names in groups)
    shape = jax.ShapeDtypeStruct(gin.shape, F32)
    if blocks == n:
        size = gin.shape[0]
        shape = jax.ShapeDtypeStruct((space * n, size // space, size // n), BF)
    args = [order, velocity, *weights, gin, *here, *own, *over, *there]
    return pl.pallas_call(
        functools.partial(border_kernel, eps, groups, beyond, space, n),
        in_specs=[smem, smem] + [vmem] * (len(args) - 2),
        out_specs=vmem,
        out_shape=shape,
        scratch_shapes=[VMEM(gin.shape, F32)],
        compiler_params=pltpu.CompilerParams(vmem_limit_bytes=16 << 20),
        cost_estimate=pl.CostEstimate(flops=1, bytes_accessed=1, transcendentals=0),
    )(*args)


def pack_kernel(jobs, rows, tiles, order, field, *refs):
    outs, sem = refs[:-1], refs[-1]
    q = order[0]
    deep = rows - 2
    copies = []
    for k, (d, kind, a, b) in enumerate(jobs):
        base = (q ^ d) * tiles * LANES
        cut = lambda t: pl.ds(pl.multiple_of(base + t * LANES, LANES), LANES)
        for t in range(tiles):
            if kind == "full":
                copies.append((field.at[:, :, cut(t)], outs[k].at[t * rows : (t + 1) * rows]))
                continue
            inside = slice(1, rows - 1)
            if t not in (0, tiles - 1):
                begin = 2 * (2 * tiles + 2 * deep) if kind == "rim" else 0
                to = slice(begin + (t - 1) * deep, begin + t * deep)
                copies.append((field.at[inside, a:b, cut(t)], outs[k].at[to]))
            if kind == "rim":
                for c in (0, 1):
                    first = c * (2 * tiles + 2 * deep)
                    half = slice(c * (b - a), (c + 1) * (b - a))
                    copies.append((field.at[0, half, cut(t)], outs[k].at[first + t]))
                    copies.append((field.at[rows - 1, half, cut(t)], outs[k].at[first + tiles + t]))
                    if t in (0, tiles - 1):
                        to = first + 2 * tiles + (deep if t else 0)
                        copies.append((field.at[inside, half, cut(t)], outs[k].at[to : to + deep]))
    copies = [pltpu.make_async_copy(src, dst, sem.at[m]) for m, (src, dst) in enumerate(copies)]
    for c in copies:
        c.start()
    for c in copies:
        c.wait()


def pack(jobs, tiles, order, field):
    rows, count, _ = field.shape
    deep = rows - 2
    shapes, pieces = [], 0
    for d, kind, a, b in jobs:
        if kind == "full":
            shapes.append((tiles * rows, count, LANES))
            pieces += tiles
        else:
            length = (tiles - 2) * deep
            pieces += tiles - 2
            if kind == "rim":
                length += 2 * (2 * tiles + 2 * deep)
                pieces += 4 * tiles + 4
            shapes.append((length, b - a, LANES))
    anywhere = pl.BlockSpec(memory_space=pl.ANY)
    return pl.pallas_call(
        functools.partial(pack_kernel, jobs, rows, tiles),
        in_specs=[pl.BlockSpec(memory_space=pltpu.SMEM), anywhere],
        out_specs=[anywhere] * len(jobs),
        out_shape=[jax.ShapeDtypeStruct(s, BF) for s in shapes],
        scratch_shapes=[pltpu.SemaphoreType.DMA((pieces,))],
        compiler_params=pltpu.CompilerParams(vmem_limit_bytes=PACK_VMEM << 20),
    )(order, field)


def first_kernel(owners, rows, tiles, order, field, *refs):
    count = len(owners)
    outs, (stage, into, out_of) = refs[:count], refs[count:]
    loads, stores = [], []
    for k, d in enumerate(owners):
        wide = pl.ds(pl.multiple_of((order[0] ^ d) * tiles * LANES, LANES), tiles * LANES)
        loads.append(pltpu.make_async_copy(field.at[:, :, wide], stage.at[k], into.at[k]))
        loads[-1].start()
    for k in range(count):
        loads[k].wait()
        for t in range(tiles):
            lanes = slice(t * LANES, (t + 1) * LANES)
            to = outs[k].at[t * rows : (t + 1) * rows]
            stores.append(
                pltpu.make_async_copy(stage.at[k, :, :, lanes], to, out_of.at[k * tiles + t])
            )
            stores[-1].start()
    for c in stores:
        c.wait()


def first_pack(owners, tiles, order, field):
    rows, count, _ = field.shape
    shape = jax.ShapeDtypeStruct((tiles * rows, count, LANES), BF)
    anywhere = pl.BlockSpec(memory_space=pl.ANY)
    return pl.pallas_call(
        functools.partial(first_kernel, owners, rows, tiles),
        in_specs=[pl.BlockSpec(memory_space=pltpu.SMEM), anywhere],
        out_specs=[anywhere] * len(owners),
        out_shape=[shape] * len(owners),
        scratch_shapes=[
            VMEM((len(owners), rows, count, tiles * LANES), BF),
            pltpu.SemaphoreType.DMA((len(owners),)),
            pltpu.SemaphoreType.DMA((len(owners) * tiles,)),
        ],
        compiler_params=pltpu.CompilerParams(vmem_limit_bytes=60 << 20),
    )(order, field)


def spread_out(total, n, space, q, count):
    share = n * count // space
    out = []
    for s in range(space):
        start = ((s * share) // count ^ q) * count + (s * share) % count
        rows = lax.dynamic_slice_in_dim(total, start, share, axis=0)
        out += [lax.dynamic_slice_in_dim(rows, (z ^ q) * count, count, axis=1) for z in range(n)]
    return jnp.stack(out)


def after(value, token):
    return lax.optimization_barrier((value, token))[0]


def local(modes, phases, velocity):
    space, n = lax.axis_size("space"), lax.axis_size("mode")
    sp, q = lax.axis_index("space"), lax.axis_index("mode")
    count, rows, plane = modes.shape
    width = plane // n
    tiles = width // LANES
    eps = 1.0 / math.sqrt(space * rows * plane)
    field = jnp.transpose(modes, (1, 0, 2))
    flip = sp & 1

    weight = jnp.where(phases == 0, 0.1, jnp.where(phases == 1, 1.0, 0.5)).astype(F32)
    w = lax.dynamic_slice_in_dim(weight, q * width, width, axis=1)[:, None, :]

    near = jnp.where(flip == 0, jnp.minimum((q + 1) * width, plane - NZ), jnp.maximum(q * width - NZ, 0))
    mine = jnp.where(flip == 0, (q + 1) * width - NZ, q * width)
    wh, wn = [
        lax.dynamic_slice_in_dim(weight, v, NZ, axis=1).reshape(rows // 2, 1, LANES)
        for v in (near, mine)
    ]

    def slab(source, owner):
        return lax.dynamic_slice_in_dim(source, owner * width, width, axis=2)

    ahead = [(i + 1, i) for i in range(space - 1)]
    above = lambda v: lax.ppermute(v, "space", ahead)
    cut = lambda v: lax.dynamic_slice_in_dim(v, q * width, width, axis=1).reshape(tiles, 1, LANES)
    weights = (wn, wh, cut(weight[rows - 1 :]), cut(above(weight[:1])))

    def swap(part, d):
        return lax.ppermute(part, "mode", [(i, i ^ d) for i in range(n)])

    relay = [(s * n + i, s * n + i - 1 + 2 * (s & 1)) for s in range(space) for i in range(n)]
    relay = [(i, j) for i, j in relay if i // n == j // n and j >= 0]
    beside = lambda v: lax.ppermute(v, ("space", "mode"), relay)
    source = jnp.clip(q + 1 - 2 * flip, 0, n - 1) ^ q
    partner = jnp.clip(q - 1 + 2 * flip, 0, n - 1) ^ q
    order = jnp.stack([q, flip, partner])
    base = dict(rows=rows, tiles=tiles, eps=eps, n=n, space=space, index=None, d=0, vmem=12)
    if n != 4:
        xs = [slab(field, q)] + [swap(slab(field, q ^ d), d) for d in range(1, n)]
        x = jnp.concatenate(xs, axis=1)
        cfg = dict(base, whole=n * count, count=n * count, n_blocks=1, old=[], vmem=40)
        x = jnp.concatenate([x[:, :, t * LANES : (t + 1) * LANES] for t in range(tiles)], axis=0)
        _, total = phase(cfg, order, velocity, w, [x], [], None, None)
        send, here, send_row, own = lines_of([x], rows, tiles, order, (0, 0, 1))
        there = beside(send).reshape(rows // 2, n, count, LANES)
        there = there[:, jnp.arange(n) ^ source].reshape(send.shape)
        total = border(
            eps, [[0]], [[0]], order, velocity, weights, total,
            [here], [own], [above(send_row)], [there], space, n,
        )
        tiles = spread_out(total, n, space, q, count)
    else:
        half = count // 2
        p1, p3 = first_pack((1, 3), tiles, order, field)
        x1, x3 = swap(p1, 1), swap(p3, 3)
        jobs = [(0, "full", 0, 0), (2, "rim", 0, half), (2, "inner", half, count)]
        x0, p2, p2b = pack(jobs, tiles, order, after(field, p3))
        front, back = swap(p2, 2), swap(p2b, 2)
        base = dict(base, whole=count, n_blocks=n)
        names, old, g = [], [], None

        halo, halo1 = halos_of(n, tiles, order, after(field, p2b))
        there, met = [halo, swap(halo1, 1)], []

        def meet(arrays, choice):
            send, here, row, own = lines_of(arrays, rows, tiles, order, choice)
            met.append((here, own, above(row)))
            there.append(beside(send))

        x0 = after(x0, weights)
        for d, x in ((0, x0), (3, x3), (1, x1)):
            if names:
                x = after(x, g)
            if d == 1:
                meet([x0, x3, x], (1, 2, 3))
            cfg = dict(base, count=count, d=d, old=list(names))
            kept, g = phase(cfg, order, velocity, w, [x], old, None, g)
            names, old = [*names, d], [*old, (x, kept)]
        front = after(front, (g, met[-1][2]))
        meet([front, x0], (0, 1, 1))
        part = dict(base, d=2, count=half, old=names, index=0)
        kept = phase(part, order, velocity, w, [front], [], None, None)
        back = after(back, (kept[1], met[-1][2]))
        part = dict(part, index=1)
        (g,) = phase(part, order, velocity, w, [front, back], old, kept, g)
        met = [list(v) for v in zip(*met)]
        g = border(
            eps, [[0, 3, 1], [2]], [[0], [1], [2], [3]], order, velocity, weights, g,
            *met, there, space, n,
        )
        tiles = g
    arrived = lax.all_to_all(tiles, ("space", "mode"), split_axis=0, concat_axis=0, tiled=True)
    return jnp.sum(arrived.astype(F32), axis=0) * eps


def solution(mesh):
    placed = (P("mode", "space", None), P("space", None), P())
    return jax.shard_map(
        local, mesh=mesh, in_specs=placed, out_specs=P("space", "mode"), check_vma=False
    )
```

```python
import functools
import math

import jax
import jax.numpy as jnp
from jax import lax
from jax.experimental import pallas as pl
from jax.experimental.pallas import tpu as pltpu
from jax.sharding import PartitionSpec as P

NZ = 64
LANES = 128
SUB = 16
PACK_VMEM = 16
PIECES = 3
BF = jnp.bfloat16
F32 = jnp.float32
VMEM = pltpu.VMEM


def product(left, right):
    return lax.dot_general(left, right, (((1,), (1,)), ((), ())), preferred_element_type=F32)


def apply_rows(i, eps, velocity, w, xs, a, tiles, rows, off, count):
    span = rows + 2
    xp, xm = eps - 0.5 * velocity[0], eps + 0.5 * velocity[0]
    yp, ym = eps - 0.5 * velocity[1], eps + 0.5 * velocity[1]
    zp, zm = eps - 0.5 * velocity[2], eps + 0.5 * velocity[2]
    lane = lax.broadcasted_iota(jnp.int32, (SUB, LANES), 1)
    low = lane < NZ
    zps = jnp.where(lane % NZ == NZ - 1, 0.0, zp)
    zms = jnp.where(lane % NZ == 0, 0.0, zm)
    own = jnp.where(low, yp, ym)
    other = jnp.where(low, ym, yp)

    def body(j, carry):
        source = pl.ds(pl.multiple_of(j * SUB, SUB), SUB)
        target = pl.ds(pl.multiple_of(j * SUB + off, SUB), SUB)
        center = [
            [xs[t * span + 2 * i + r, source, :].astype(F32) for t in range(tiles)] for r in range(4)
        ]
        for r in (0, 1):
            mid = center[r + 1]
            turned = [pltpu.roll(c, NZ, 1) for c in mid]
            for t in range(tiles):
                c = mid[t]
                behind = turned[t + 1] if t + 1 < tiles else jnp.zeros_like(c)
                before = turned[t - 1] if t > 0 else jnp.zeros_like(c)
                value = xp * center[r + 2][t] + xm * center[r][t]
                value = value + own * turned[t] + other * jnp.where(low, before, behind)
                value = value + zps * pltpu.roll(c, LANES - 1, 1) + zms * pltpu.roll(c, 1, 1)
                value = (value - (6.0 * eps) * c) * w[2 * i + r, :, t * LANES : (t + 1) * LANES]
                a[t * rows + 2 * i + r, target, :] = value.astype(BF)
        return carry

    lax.fori_loop(0, count // SUB, body, 0, unroll=4)


def phase_kernel(cfg, *refs):
    refs = list(refs)
    take = lambda k: [refs.pop(0) for _ in range(k)]
    d, count, whole, index = cfg["d"], cfg["count"], cfg["whole"], cfg["index"]
    rows, tiles = cfg["rows"], cfg["tiles"]
    steps, span = rows // 2, rows + 2
    order, velocity, w = take(3)
    parts = take(cfg["n_parts"])
    old = [take(2) for _ in range(cfg["n_old"])]
    prev = take(2) if index == 1 else None
    gin = take(1)[0] if cfg["gin"] else None
    xo = take(1)[0] if index == 0 else None
    a = take(1)[0] if index != 1 else None
    gout = take(1)[0] if index != 0 else None
    if index == 1:
        (a,) = take(1)
    xs = take(1)[0]
    t2 = take(1)[0] if index != 0 else None
    t1 = take(1)[0] if old and index != 0 else None

    if index is not None:
        rim, inner = parts[0], parts[-1]
        deep = rows - 2
        begin = inner.shape[0] - (tiles - 2) * deep
        base = index * (2 * tiles + 2 * deep)
        sides = (base + 2 * tiles, base + 2 * tiles + deep)
    for t in range(tiles):
        xs[t * span] = jnp.zeros_like(xs[0])
        xs[t * span + rows + 1] = jnp.zeros_like(xs[0])
        if index is not None:
            xs[t * span + 1] = rim[base + t]
            xs[t * span + rows] = rim[base + tiles + t]
            if t in (0, tiles - 1):
                first = sides[t // (tiles - 1)]
                xs[t * span + 2 : t * span + rows] = rim[first : first + deep]
            else:
                xs[t * span + 2 : t * span + rows] = inner[begin + (t - 1) * deep : begin + t * deep]
        else:
            xs[t * span + 1 : t * span + rows + 1] = parts[0][t * rows : (t + 1) * rows]

    def stencil(i, carry):
        apply_rows(i, cfg["eps"], velocity, w, xs, a, tiles, rows, 0, count)
        return carry

    lax.fori_loop(0, steps, stencil, 0)
    if index == 0:
        for t in range(tiles):
            xo[t * rows : (t + 1) * rows] = xs[t * span + 1 : t * span + rows + 1]
        return

    t2[...] = jnp.zeros_like(t2)
    if t1 is not None:
        t1[...] = jnp.zeros_like(t1)

    def body(i, carry):
        pairs = [(r, t) for r in (0, 1) for t in range(tiles)]
        picks = [t * rows + 2 * i + r for r, t in pairs]
        join = lambda pieces: jnp.concatenate(pieces, axis=1)
        wide = lambda ref: join([ref[k] for k in picks])
        new = join([xs[t * span + 2 * i + r + 1] for r, t in pairs])
        mark = wide(a)
        if prev is not None:
            new = jnp.concatenate([wide(prev[0]), new], axis=0)
            mark = jnp.concatenate([wide(prev[1]), mark], axis=0)
        t2[...] += product(jnp.concatenate([wide(ox) for ox, _ in old] + [new], axis=0), mark)
        if old:
            t1[...] += product(jnp.concatenate([wide(oa) for _, oa in old], axis=0), new)
        return carry

    lax.fori_loop(0, steps, body, 0)

    gout[...] = jnp.zeros_like(gout) if gin is None else gin[...]
    block = lambda k: slice(k * whole, (k + 1) * whole)
    for k, o in enumerate([*cfg["old"], d]):
        gout[block(o), block(d)] += t2[block(k), :]
        if o != d:
            gout[block(d), block(o)] += t1[block(k), :].T


def phase(cfg, order, velocity, w, parts, old, prev, gin):
    rows, tiles, whole, count = cfg["rows"], cfg["tiles"], cfg["whole"], cfg["count"]
    size, index = cfg["n_blocks"] * whole, cfg["index"]
    kept = jax.ShapeDtypeStruct((tiles * rows, count, LANES), BF)
    total = jax.ShapeDtypeStruct((size, size), F32)
    args = [order, velocity, w, *parts]
    for group in [*old, *([prev] if prev is not None else [])]:
        args += list(group)
    if gin is not None:
        args.append(gin)
    out_shape = {None: [kept, total], 0: [kept, kept], 1: [total]}[index]
    scratch = [VMEM(kept.shape, BF)] if index == 1 else []
    scratch.append(VMEM((tiles * (rows + 2), count, LANES), BF))
    if index != 0:
        scratch.append(VMEM(((len(old) + 1) * whole, whole), F32))
        if old:
            scratch.append(VMEM((len(old) * whole, whole), F32))
    cfg = dict(cfg, n_parts=len(parts), n_old=len(old), gin=gin is not None)
    vmem = pl.BlockSpec(memory_space=VMEM)
    smem = pl.BlockSpec(memory_space=pltpu.SMEM)
    return pl.pallas_call(
        functools.partial(phase_kernel, cfg),
        in_specs=[smem, smem] + [vmem] * (len(args) - 2),
        out_specs=[vmem] * len(out_shape),
        out_shape=out_shape,
        scratch_shapes=scratch,
        compiler_params=pltpu.CompilerParams(vmem_limit_bytes=cfg["vmem"] << 20),
        cost_estimate=pl.CostEstimate(flops=1, bytes_accessed=1, transcendentals=0),
    )(*args)


def line_kernel(rows, tiles, choice, order, *refs):
    ins, (near, far, near_row, far_row) = refs[:-4], refs[-4:]
    deep = rows - 2
    keep = order[1] == 0

    def tile_row(ref, row, t, c):
        if c is None:
            return ref[t * rows + row].astype(F32)
        base = c * (2 * tiles + 2 * deep)
        if row in (0, rows - 1):
            return ref[base + (tiles if row else 0) + t].astype(F32)
        return ref[base + 2 * tiles + (deep if t else 0) + row - 1].astype(F32)

    def parts_of(ref):
        return [(ref, None)] if ref.shape[0] == tiles * rows else [(ref, 0), (ref, 1)]

    def line(ref, c, i, first):
        t = 0 if first else tiles - 1
        low = lax.broadcasted_iota(jnp.int32, (ref.shape[1], LANES), 1) < NZ
        one, two = tile_row(ref, 2 * i, t, c), tile_row(ref, 2 * i + 1, t, c)
        if first:
            return jnp.where(low, one, pltpu.roll(two, NZ, 1))
        return jnp.where(low, pltpu.roll(one, NZ, 1), two)

    start = 0
    for ref in ins[: choice[2]]:
        for ref, c in parts_of(ref):
            modes = slice(start, start + ref.shape[1])
            start += ref.shape[1]
            for t in range(tiles):
                near_row[t, modes, :] = tile_row(ref, 0, t, c).astype(BF)
                far_row[t, modes, :] = tile_row(ref, rows - 1, t, c).astype(BF)
            for i in range(rows // 2):
                value = jnp.where(keep, line(ref, c, i, False), line(ref, c, i, True))
                far[i, modes, :] = value.astype(BF)

    def send(ref):
        start = 0
        for ref, c in parts_of(ref):
            modes = slice(start, start + ref.shape[1])
            start += ref.shape[1]
            for i in range(rows // 2):
                value = jnp.where(keep, line(ref, c, i, True), line(ref, c, i, False))
                near[i, modes, :] = value.astype(BF)

    if choice[0] == choice[1]:
        send(ins[choice[0]])
    else:
        pl.when(order[2] == 1)(lambda: send(ins[choice[0]]))
        pl.when(order[2] != 1)(lambda: send(ins[choice[1]]))


def lines_of(arrays, rows, tiles, order, choice):
    size = lambda v: v.shape[1] * (1 if v.shape[0] == tiles * rows else 2)
    modes = sum(size(v) for v in arrays[: choice[2]])
    vmem = pl.BlockSpec(memory_space=VMEM)
    lines = lambda m: jax.ShapeDtypeStruct((rows // 2, m, LANES), BF)
    row = jax.ShapeDtypeStruct((tiles, modes, LANES), BF)
    return pl.pallas_call(
        functools.partial(line_kernel, rows, tiles, choice),
        in_specs=[pl.BlockSpec(memory_space=pltpu.SMEM)] + [vmem] * len(arrays),
        out_specs=[vmem] * 4,
        out_shape=[lines(size(arrays[choice[0]])), lines(modes), row, row],
        compiler_params=pltpu.CompilerParams(vmem_limit_bytes=12 << 20),
        cost_estimate=pl.CostEstimate(flops=1, bytes_accessed=1, transcendentals=0),
    )(order, *arrays)


def halo_kernel(n, tiles, order, field, *refs):
    outs, (line, sem) = refs[:2], refs[2:]
    q, flip = order[0], order[1]
    copies = []
    for d in (0, 1):
        owner = q ^ d
        at = jnp.where(
            flip == 0,
            jnp.minimum((owner + 1) * tiles, n * tiles - 1),
            jnp.maximum(owner * tiles - 1, 0),
        )
        at = pl.ds(pl.multiple_of(at * LANES, LANES), LANES)
        copies.append(pltpu.make_async_copy(field.at[:, :, at], line.at[d], sem.at[d]))
        copies[-1].start()
    low = lax.broadcasted_iota(jnp.int32, line.shape[2:], 1) < NZ
    for d in (0, 1):
        copies[d].wait()
        owner = q ^ d
        none = jnp.where(flip == 0, owner == n - 1, owner == 0)
        for i in range(line.shape[1] // 2):
            one, two = line[d, 2 * i].astype(F32), line[d, 2 * i + 1].astype(F32)
            front = jnp.where(low, one, pltpu.roll(two, NZ, 1))
            back = jnp.where(low, pltpu.roll(one, NZ, 1), two)
            value = jnp.where(flip == 0, front, back)
            outs[d][i] = jnp.where(none, 0.0, value).astype(BF)


def halos_of(n, tiles, order, field):
    rows, count, _ = field.shape
    shape = jax.ShapeDtypeStruct((rows // 2, count, LANES), BF)
    return pl.pallas_call(
        functools.partial(halo_kernel, n, tiles),
        in_specs=[pl.BlockSpec(memory_space=pltpu.SMEM), pl.BlockSpec(memory_space=pl.ANY)],
        out_specs=[pl.BlockSpec(memory_space=VMEM)] * 2,
        out_shape=[shape] * 2,
        scratch_shapes=[VMEM((2, rows, count, LANES), BF), pltpu.SemaphoreType.DMA((2,))],
        compiler_params=pltpu.CompilerParams(vmem_limit_bytes=12 << 20),
        cost_estimate=pl.CostEstimate(flops=1, bytes_accessed=1, transcendentals=0),
    )(order, field)


def border_kernel(eps, groups, beyond, space, n, order, velocity, wn, wh, wr, wx, gin, *refs):
    count = len(groups)
    here, own, over = refs[:count], refs[count : 2 * count], refs[2 * count : 3 * count]
    there, (out, g) = refs[3 * count : -2], refs[-2:]
    xp, xm = eps - 0.5 * velocity[0], eps + 0.5 * velocity[0]
    yp, ym = eps - 0.5 * velocity[1], eps + 0.5 * velocity[1]
    toward = jnp.where(order[1] == 0, yp, ym)
    back = jnp.where(order[1] == 0, ym, yp)
    blocks = sum(len(names) for names in groups)
    size = g.shape[0] // blocks

    def find(refs, d, i, groups=groups):
        for names, ref in zip(groups, refs):
            if d in names:
                k = names.index(d)
                return ref[i, k * size : (k + 1) * size, :]

    def every(refs, i, groups=groups):
        return jnp.concatenate([find(refs, d, i, groups) for d in range(blocks)], axis=0)

    left, right = [], []
    for k in range(wn.shape[0]):
        mine = every(here, k)
        other = every(there, k, beyond).astype(F32)
        left += [mine, other.astype(BF)]
        right += [(wn[k] * (toward * other)).astype(BF), (wh[k] * (back * mine.astype(F32))).astype(BF)]
    for t in range(wr.shape[0]):
        mine, other = every(own, t), every(over, t)
        left += [mine, other]
        right += [
            (wr[t] * (xp * other.astype(F32))).astype(BF),
            (wx[t] * (xm * mine.astype(F32))).astype(BF),
        ]
    total = gin[...]
    for k in range(0, len(left), 4):
        total = total + product(
            jnp.concatenate(left[k : k + 4], axis=1), jnp.concatenate(right[k : k + 4], axis=1)
        )
    g[...] = total
    if blocks == n:
        q = order[0]
        share = out.shape[1]
        per = size // share
        for s in range(space):
            first = pl.multiple_of(((s // per) ^ q) * size + (s % per) * share, share)
            for z in range(n):
                start = pl.multiple_of((z ^ q) * size, size)
                out[s * n + z] = g[pl.ds(first, share), pl.ds(start, size)].astype(out.dtype)
    else:
        out[...] = total


def border(eps, groups, beyond, order, velocity, weights, gin, here, own, over, there, space, n):
    vmem = pl.BlockSpec(memory_space=VMEM)
    smem = pl.BlockSpec(memory_space=pltpu.SMEM)
    blocks = sum(len(names) for names in groups)
    shape = jax.ShapeDtypeStruct(gin.shape, F32)
    if blocks == n:
        size = gin.shape[0]
        shape = jax.ShapeDtypeStruct((space * n, size // space, size // n), BF)
    args = [order, velocity, *weights, gin, *here, *own, *over, *there]
    return pl.pallas_call(
        functools.partial(border_kernel, eps, groups, beyond, space, n),
        in_specs=[smem, smem] + [vmem] * (len(args) - 2),
        out_specs=vmem,
        out_shape=shape,
        scratch_shapes=[VMEM(gin.shape, F32)],
        compiler_params=pltpu.CompilerParams(vmem_limit_bytes=16 << 20),
        cost_estimate=pl.CostEstimate(flops=1, bytes_accessed=1, transcendentals=0),
    )(*args)


def pack_kernel(jobs, rows, tiles, order, field, *refs):
    outs, sem = refs[:-1], refs[-1]
    q = order[0]
    deep = rows - 2
    copies = []
    for k, (d, kind, a, b) in enumerate(jobs):
        base = (q ^ d) * tiles * LANES
        cut = lambda t: pl.ds(pl.multiple_of(base + t * LANES, LANES), LANES)
        for t in range(tiles):
            if kind == "full":
                copies.append((field.at[:, :, cut(t)], outs[k].at[t * rows : (t + 1) * rows]))
                continue
            inside = slice(1, rows - 1)
            if kind == "inner" and t not in (0, tiles - 1):
                to = slice((t - 1) * deep, t * deep)
                copies.append((field.at[inside, a:b, cut(t)], outs[k].at[to]))
            if kind == "rim":
                for c in (0, 1):
                    first = c * (2 * tiles + 2 * deep)
                    half = slice(c * (b - a), (c + 1) * (b - a))
                    copies.append((field.at[0, half, cut(t)], outs[k].at[first + t]))
                    copies.append((field.at[rows - 1, half, cut(t)], outs[k].at[first + tiles + t]))
                    if t in (0, tiles - 1):
                        to = first + 2 * tiles + (deep if t else 0)
                        copies.append((field.at[inside, half, cut(t)], outs[k].at[to : to + deep]))
    copies = [pltpu.make_async_copy(src, dst, sem.at[m]) for m, (src, dst) in enumerate(copies)]
    for c in copies:
        c.start()
    for c in copies:
        c.wait()


def pack(jobs, tiles, order, field):
    rows, count, _ = field.shape
    deep = rows - 2
    shapes, pieces = [], 0
    for d, kind, a, b in jobs:
        if kind == "full":
            shapes.append((tiles * rows, count, LANES))
            pieces += tiles
        else:
            length = (tiles - 2) * deep if kind == "inner" else 2 * (2 * tiles + 2 * deep)
            pieces += tiles - 2 if kind == "inner" else 4 * tiles + 4
            shapes.append((length, b - a, LANES))
    anywhere = pl.BlockSpec(memory_space=pl.ANY)
    return pl.pallas_call(
        functools.partial(pack_kernel, jobs, rows, tiles),
        in_specs=[pl.BlockSpec(memory_space=pltpu.SMEM), anywhere],
        out_specs=[anywhere] * len(jobs),
        out_shape=[jax.ShapeDtypeStruct(s, BF) for s in shapes],
        scratch_shapes=[pltpu.SemaphoreType.DMA((pieces,))],
        compiler_params=pltpu.CompilerParams(vmem_limit_bytes=PACK_VMEM << 20),
    )(order, field)


def first_kernel(owners, rows, tiles, order, field, *refs):
    count = len(owners)
    outs, (stage, into, out_of) = refs[:count], refs[count:]
    loads, stores = [], []
    for k, d in enumerate(owners):
        wide = pl.ds(pl.multiple_of((order[0] ^ d) * tiles * LANES, LANES), tiles * LANES)
        for c in range(PIECES):
            some = slice(c * rows // PIECES, (c + 1) * rows // PIECES)
            loads.append(
                pltpu.make_async_copy(
                    field.at[some, :, wide], stage.at[k, some], into.at[k * PIECES + c]
                )
            )
            loads[-1].start()
    for k in range(count):
        for c in range(PIECES):
            a, b = c * rows // PIECES, (c + 1) * rows // PIECES
            loads[k * PIECES + c].wait()
            for t in range(tiles):
                lanes = slice(t * LANES, (t + 1) * LANES)
                to = outs[k].at[t * rows + a : t * rows + b]
                sem = out_of.at[(k * PIECES + c) * tiles + t]
                stores.append(pltpu.make_async_copy(stage.at[k, a:b, :, lanes], to, sem))
                stores[-1].start()
    for c in stores:
        c.wait()


def first_pack(owners, tiles, order, field):
    rows, count, _ = field.shape
    shape = jax.ShapeDtypeStruct((tiles * rows, count, LANES), BF)
    anywhere = pl.BlockSpec(memory_space=pl.ANY)
    return pl.pallas_call(
        functools.partial(first_kernel, owners, rows, tiles),
        in_specs=[pl.BlockSpec(memory_space=pltpu.SMEM), anywhere],
        out_specs=[anywhere] * len(owners),
        out_shape=[shape] * len(owners),
        scratch_shapes=[
            VMEM((len(owners), rows, count, tiles * LANES), BF),
            pltpu.SemaphoreType.DMA((len(owners) * PIECES,)),
            pltpu.SemaphoreType.DMA((len(owners) * PIECES * tiles,)),
        ],
        compiler_params=pltpu.CompilerParams(vmem_limit_bytes=60 << 20),
    )(order, field)


def spread_out(total, n, space, q, count):
    share = n * count // space
    out = []
    for s in range(space):
        start = ((s * share) // count ^ q) * count + (s * share) % count
        rows = lax.dynamic_slice_in_dim(total, start, share, axis=0)
        out += [lax.dynamic_slice_in_dim(rows, (z ^ q) * count, count, axis=1) for z in range(n)]
    return jnp.stack(out)


def after(value, token):
    return lax.optimization_barrier((value, token))[0]


def local(modes, phases, velocity):
    space, n = lax.axis_size("space"), lax.axis_size("mode")
    sp, q = lax.axis_index("space"), lax.axis_index("mode")
    count, rows, plane = modes.shape
    width = plane // n
    tiles = width // LANES
    eps = 1.0 / math.sqrt(space * rows * plane)
    field = jnp.transpose(modes, (1, 0, 2))
    flip = sp & 1

    weight = jnp.where(phases == 0, 0.1, jnp.where(phases == 1, 1.0, 0.5)).astype(F32)
    w = lax.dynamic_slice_in_dim(weight, q * width, width, axis=1)[:, None, :]

    near = jnp.where(flip == 0, jnp.minimum((q + 1) * width, plane - NZ), jnp.maximum(q * width - NZ, 0))
    mine = jnp.where(flip == 0, (q + 1) * width - NZ, q * width)
    wh, wn = [
        lax.dynamic_slice_in_dim(weight, v, NZ, axis=1).reshape(rows // 2, 1, LANES)
        for v in (near, mine)
    ]

    def slab(source, owner):
        return lax.dynamic_slice_in_dim(source, owner * width, width, axis=2)

    ahead = [(i + 1, i) for i in range(space - 1)]
    above = lambda v: lax.ppermute(v, "space", ahead)
    cut = lambda v: lax.dynamic_slice_in_dim(v, q * width, width, axis=1).reshape(tiles, 1, LANES)
    weights = (wn, wh, cut(weight[rows - 1 :]), cut(above(weight[:1])))

    def swap(part, d):
        return lax.ppermute(part, "mode", [(i, i ^ d) for i in range(n)])

    relay = [(s * n + i, s * n + i - 1 + 2 * (s & 1)) for s in range(space) for i in range(n)]
    relay = [(i, j) for i, j in relay if i // n == j // n and j >= 0]
    beside = lambda v: lax.ppermute(v, ("space", "mode"), relay)
    source = jnp.clip(q + 1 - 2 * flip, 0, n - 1) ^ q
    partner = jnp.clip(q - 1 + 2 * flip, 0, n - 1) ^ q
    order = jnp.stack([q, flip, partner])
    base = dict(rows=rows, tiles=tiles, eps=eps, n=n, space=space, index=None, d=0, vmem=12)
    if n != 4:
        xs = [slab(field, q)] + [swap(slab(field, q ^ d), d) for d in range(1, n)]
        x = jnp.concatenate(xs, axis=1)
        cfg = dict(base, whole=n * count, count=n * count, n_blocks=1, old=[], vmem=40)
        x = jnp.concatenate([x[:, :, t * LANES : (t + 1) * LANES] for t in range(tiles)], axis=0)
        _, total = phase(cfg, order, velocity, w, [x], [], None, None)
        send, here, send_row, own = lines_of([x], rows, tiles, order, (0, 0, 1))
        there = beside(send).reshape(rows // 2, n, count, LANES)
        there = there[:, jnp.arange(n) ^ source].reshape(send.shape)
        total = border(
            eps, [[0]], [[0]], order, velocity, weights, total,
            [here], [own], [above(send_row)], [there], space, n,
        )
        tiles = spread_out(total, n, space, q, count)
    else:
        half = count // 2
        p3, p1 = first_pack((3, 1), tiles, order, field)
        x3, x1 = swap(p3, 3), swap(p1, 1)
        jobs = [(0, "full", 0, 0), (2, "rim", 0, half), (2, "inner", 0, half), (2, "inner", half, count)]
        x0, p2, p2a, p2b = pack(jobs, tiles, order, after(field, p3))
        rim = swap(p2, 2)
        front, back = swap(p2a, 2), swap(p2b, 2)
        base = dict(base, whole=count, n_blocks=n)
        names, old, g = [], [], None

        halo, halo1 = halos_of(n, tiles, order, after(field, p2b))
        there, met = [halo, swap(halo1, 1)], []

        def meet(arrays, choice):
            send, here, row, own = lines_of(arrays, rows, tiles, order, choice)
            met.append((here, own, above(row)))
            there.append(beside(send))

        x0 = after(x0, weights)
        for d, x in ((0, x0), (3, x3), (1, x1)):
            if names:
                x = after(x, g)
            if d == 1:
                meet([x0, x3, x], (1, 2, 3))
            cfg = dict(base, count=count, d=d, old=list(names))
            kept, g = phase(cfg, order, velocity, w, [x], old, None, g)
            names, old = [*names, d], [*old, (x, kept)]
        rim = after(rim, (g, met[-1][2]))
        meet([rim, x0], (0, 1, 1))
        front = after(front, (g, met[-1][2]))
        part = dict(base, d=2, count=half, old=names, index=0)
        kept = phase(part, order, velocity, w, [rim, front], [], None, None)
        back = after(back, (kept[1], met[-1][2]))
        part = dict(part, index=1)
        (g,) = phase(part, order, velocity, w, [rim, back], old, kept, g)
        met = [list(v) for v in zip(*met)]
        g = border(
            eps, [[0, 3, 1], [2]], [[0], [1], [2], [3]], order, velocity, weights, g,
            *met, there, space, n,
        )
        tiles = g
    arrived = lax.all_to_all(tiles, ("space", "mode"), split_axis=0, concat_axis=0, tiled=True)
    return jnp.sum(arrived.astype(F32), axis=0) * eps


def solution(mesh):
    placed = (P("mode", "space", None), P("space", None), P())
    return jax.shard_map(
        local, mesh=mesh, in_specs=placed, out_specs=P("space", "mode"), check_vma=False
    )
```
